256 devices in a mesh: blk: 16 (over y_lo, z), section: 8 (over x, core), tp: 2 (over y_hi).
Axes of the slice: x: 4, y: 4 (y_hi: 2, y_lo: 2; y = y_hi * 2 + y_lo), z: 8, core: 2. Of those that a mesh axis runs over, the one named last changes fastest.
Arguments:
- queries: bfloat16 [16384, 1280], P('blk', ('section', 'tp')), may hold values from -180 to 180
- keys: bfloat16 [16384, 1280], P('blk', ('section', 'tp')), may hold values from -6 to 6
- values: bfloat16 [16384, 1280], P('blk', ('section', 'tp')), may hold values from -6 to 6
- segment_ids: int32 [16384], P('blk'), may hold values from 0 to 7, never falling along the last dimension, each value on 1 to 9216 neighbouring positions
- out_weight: bfloat16 [1280, 1280], P(('section', 'tp')), may hold values from -0.15625 to 0.15625
- norm_gain: float32 [1280], replicated, may hold values from 0.1 to 1.9
- norm_bias: float32 [1280], replicated, may hold values from -3 to 3
- proj_weight: bfloat16 [5120, 5120], P(None, ('section', 'tp')), may hold values from -0.078125 to 0.078125
- proj_bias: float32 [5120], P(('section', 'tp')), may hold values from -3 to 3
Outputs:
- projected: bfloat16 [4096, 5120], P('blk', ('section', 'tp'))
The draws below stay inside these ranges and needn't reach their ends.
Inputs may be any that keep to these rules, and one draw needn't show every extreme that they name: `segment_ids`: image numbers never fall along the patch order, so each image covers consecutive patches; one image covers exactly 9216 patches.
All inputs are finite; a program needn't handle non-finite values.
Results may differ from the reference program's by a relative error of at most 0.02.
Values may be sent and summed in bfloat16 or wider, within the bound.
No kernel may reach another device: no remote copies, remote signals or barrier semaphores. Data moves between devices by JAX's collectives and lax.ppermute only.
A program may use at most 64 MiB of HBM per device.

```python
import math
import jax
import jax.numpy as jnp
import numpy as np
from jax import lax

P_DEV = 1024
HDIM = 80
DV = 1280
PW = 5120
CHARTS = 8
PATCH = 16384
HEADS = 16
TOK = 4096


def final_keys(key):
    drawn = jax.random.normal(jax.random.fold_in(key, 21), (PATCH, HEADS * HDIM), jnp.float32)
    drawn = jnp.clip(drawn, -6.0, 6.0)
    return drawn


def draw_keys(key, part):
    return final_keys(key).astype(jnp.bfloat16)


def draw_queries(key, part):
    drawn = 2.0 * jax.random.normal(jax.random.fold_in(key, 31), (PATCH, HEADS * HDIM), jnp.float32)
    drawn = jnp.clip(drawn, -12.0, 12.0)
    return drawn.astype(jnp.bfloat16)


def levels(key, shape, pieces, least, top_value):
    def one(position, blocks):
        steps = jax.random.uniform(jax.random.fold_in(jax.random.fold_in(key, 6), position), (blocks,), jnp.float32, least / len(pieces), top_value / len(pieces))
        return jnp.repeat(jnp.exp(steps), shape[position] // blocks).reshape((-1,) + (1,) * (len(shape) - position - 1))

    gain = one(*pieces[0])
    for cut in pieces[1:]:
        gain = gain * one(*cut)
    return gain


def split_up(count, total, limit, slope):
    loads = [(1 << 20) // math.isqrt(rank ** slope) + 1 for rank in range(2, count + 1)]
    surplus, given = total - limit - (count - 1), [1] * (count - 1)
    while surplus > 0:
        free = [i for i in range(count - 1) if given[i] < limit]
        mass, budget = sum([loads[i] for i in free]), surplus
        for i in free:
            more = min(limit - given[i], max(1, budget * loads[i] // mass), surplus)
            given[i] = given[i] + more
            surplus = surplus - more
    return np.array([limit] + given)


def ragged(key, number_of, total, limit, slope):
    if number_of == 2:
        one = jax.random.randint(key, (), max(1, total - limit), min(limit, total - 1) + 1)
        return jnp.stack([one, total - one])
    lengths = jnp.asarray(split_up(number_of, total, limit, slope), jnp.int32)
    pairs = (number_of - 1) // 2
    donor, sink = lengths[1:1 + 2 * pairs:2], lengths[2:2 + 2 * pairs:2]
    slack = jnp.minimum(donor - 1, limit - sink)
    shifted = jax.random.randint(jax.random.fold_in(key, 1), (pairs,), 0, 1 << 20) % (slack + 1)
    lengths = lengths.at[1:1 + 2 * pairs:2].set(donor - shifted).at[2:2 + 2 * pairs:2].set(sink + shifted)
    return lengths[jax.random.permutation(jax.random.fold_in(key, 2), number_of)]


def normal_values(stream_key, shape, scale, bound, shards=(), dtype=jnp.bfloat16):
    result = jax.random.normal(stream_key, shape, jnp.float32) * scale
    if len(shards) > 0:
        result = levels(stream_key, shape, shards, -0.22, 0.18) * result
    return jnp.clip(result, min=-bound, max=bound).astype(dtype)


def setup_inputs(seed: int = 0) -> dict:
    arg_keys = jax.random.split(jax.random.key(seed), 10)
    return {
        "queries": draw_queries(jax.random.fold_in(arg_keys[9], 71), 0),
        "keys": draw_keys(jax.random.fold_in(arg_keys[9], 71), 0),
        "values": normal_values(arg_keys[2], (PATCH, HEADS * HDIM), 1.0, 6.0, ((0, 16), (1, 16))),
        "segment_ids": jnp.searchsorted(jnp.cumsum(ragged(arg_keys[3], CHARTS, PATCH, PATCH // 2 + P_DEV, 0)), jnp.arange(PATCH), side="right").astype(jnp.int32),
        "out_weight": normal_values(arg_keys[4], (HEADS * HDIM, DV), (HEADS * HDIM) ** -0.5, 0.15625, ((0, 16),)),
        "norm_gain": jnp.clip(1.0 + 0.18 * jax.random.normal(arg_keys[5], (DV,), jnp.float32), 0.1, 1.9),
        "norm_bias": normal_values(arg_keys[6], (DV,), 0.5, 3.0, (), jnp.float32),
        "proj_weight": normal_values(arg_keys[7], (4 * DV, PW), (4 * DV) ** -0.5, 0.078125, ((1, 16),)),
        "proj_bias": normal_values(arg_keys[8], (PW,), 0.5, 3.0, ((0, 16),), jnp.float32),
    }


EPSILON = 1e-06

def head_attention(query_head, key_head, value_head, segment_ids):
    block_rows = math.gcd(PATCH, 1024)
    query_blocks = query_head.reshape(PATCH // block_rows, block_rows, HDIM)
    chart_blocks = segment_ids.reshape(PATCH // block_rows, block_rows)
    score_scale = HDIM ** (-0.5)

    def one_block(pair):
        query_part, chart_part = pair
        scores = jnp.dot(query_part, key_head.T, preferred_element_type=jnp.float32) * score_scale
        same_chart = chart_part[:, None] == segment_ids[None, :]
        scores = jnp.where(same_chart, scores, -1e+30)
        row_max = lax.optimization_barrier(jnp.max(scores, axis=1, keepdims=True))
        weights = jnp.where(same_chart, jnp.exp(scores - row_max), 0.0)
        row_sum = lax.optimization_barrier(jnp.sum(weights, axis=1, keepdims=True))
        gathered = jnp.dot(weights.astype(jnp.bfloat16), value_head, preferred_element_type=jnp.float32)
        return gathered / row_sum
    return lax.map(one_block, (query_blocks, chart_blocks)).reshape(PATCH, HDIM)

def reference(queries, keys, values, segment_ids, out_weight, norm_gain, norm_bias, proj_weight, proj_bias):
    query_heads = queries.reshape(PATCH, HEADS, HDIM).transpose(1, 0, 2)
    key_heads = keys.reshape(PATCH, HEADS, HDIM).transpose(1, 0, 2)
    value_heads = values.reshape(PATCH, HEADS, HDIM).transpose(1, 0, 2)

    def per_head(triple):
        return head_attention(triple[0], triple[1], triple[2], segment_ids)
    outputs = lax.map(per_head, (query_heads, key_heads, value_heads))
    attended = outputs.transpose(1, 0, 2).reshape(PATCH, HEADS * HDIM).astype(jnp.bfloat16)
    encoded = jnp.dot(attended, out_weight, preferred_element_type=jnp.float32).astype(jnp.bfloat16)
    rows = encoded.astype(jnp.float32)
    centre = lax.optimization_barrier(jnp.mean(rows, axis=1, keepdims=True))
    spread = lax.optimization_barrier(jnp.mean(jnp.square(rows - centre), axis=1, keepdims=True))
    normed = ((rows - centre) * lax.rsqrt(spread + EPSILON) * norm_gain + norm_bias).astype(jnp.bfloat16)
    merged = normed.reshape(TOK, 4 * DV)
    linear = jnp.dot(merged, proj_weight, preferred_element_type=jnp.float32) + proj_bias
    return jax.nn.gelu(linear, approximate=False).astype(jnp.bfloat16)
```

```python
import functools

import jax
import jax.numpy as jnp
from jax import lax
from jax.experimental import pallas as pl
from jax.experimental.pallas import tpu as pltpu
from jax.sharding import PartitionSpec as P

HDIM = 80
EPSILON = 1e-06
EXP2_SCALE = 1.4426950408889634 * HDIM ** (-0.5)
MASKED = -1e30
NO_MAX = -1e20
KEY_PARTNERS = (0, 1, 8, 9)
QUERY_PARTNERS = (0, 4, 10, 14)
f32, bf16 = jnp.float32, jnp.bfloat16
GROUP = ("section", "tp")
IN_VMEM = pl.BlockSpec(memory_space=pltpu.VMEM)
IN_SMEM = pl.BlockSpec(memory_space=pltpu.SMEM)


def pack_kernel(queries, keys, values, ids, query_block, key_block):
    count = queries.shape[1]
    id_row = ids[...].astype(f32)
    zeros = jnp.zeros((6, count), f32)
    query_block[0:80, :] = queries[...]
    query_block[80:88, :] = jnp.concatenate([id_row, id_row, zeros], axis=0).astype(bf16)
    key_block[0:80, :] = keys[...]
    key_block[80:160, :] = values[...]
    key_block[160:168, :] = jnp.concatenate([jnp.ones_like(id_row), id_row, zeros], axis=0).astype(bf16)


def pack(queries, keys, values, ids):
    count = queries.shape[1]
    return pl.pallas_call(
        pack_kernel,
        out_shape=[
            jax.ShapeDtypeStruct((88, count), bf16),
            jax.ShapeDtypeStruct((168, count), bf16),
        ],
        in_specs=[IN_VMEM] * 4,
        out_specs=[IN_VMEM] * 2,
        compiler_params=pltpu.CompilerParams(vmem_limit_bytes=4 << 20),
        name="pack",
    )(queries, keys, values, ids)


def attend_block(query, held_k, held_v, limits, which, row_max, total):
    count = query.shape[1]
    tiles, sub = 2, 256
    row_max[...] = jnp.full_like(row_max, NO_MAX)
    total[...] = jnp.zeros_like(total)
    q_low, q_high = limits[which, 0], limits[which, 3]

    def tile(kb, start, tile_keys, masked):
        rows = pl.ds(start, tile_keys)
        key_tile = held_k[kb, rows, :]
        value_tile = held_v[kb, :, rows]
        if masked:
            key_ids = jnp.broadcast_to(value_tile[80:88, :].T.astype(f32)[:, 1:2], (tile_keys, sub))

        def score(j):
            columns = slice(j * sub, (j + 1) * sub)
            found = jnp.dot(key_tile, query[0:80, columns], preferred_element_type=f32)
            if masked:
                query_ids = query[80:88, columns].astype(f32)[0:1, :]
                found = jnp.where(key_ids == query_ids, found, MASKED)
            return found

        scores = score(0)
        for j in range(count // sub):
            following = score(j + 1) if (j + 1) * sub < count else None
            columns = slice(j * sub, (j + 1) * sub)
            old = row_max[:, columns]
            new = jnp.maximum(old, jnp.max(scores, axis=0, keepdims=True))
            weights = jnp.exp2((scores - new) * EXP2_SCALE).astype(bf16)
            rescale = jnp.exp2((old - new) * EXP2_SCALE)
            total[:, columns] = total[:, columns] * rescale + jnp.dot(
                value_tile, weights, preferred_element_type=f32
            )
            row_max[:, columns] = new
            scores = following

    def key_block_step(kb, unused):
        low, high = limits[4 + kb, 0], limits[4 + kb, 3]
        whole = jnp.logical_and(jnp.logical_and(low == high, q_low == q_high), low == q_low)

        @pl.when(whole)
        def _():
            tile(kb, 0, count, False)

        @pl.when(jnp.logical_not(whole))
        def _():
            def half(t, unused):
                low, high = limits[4 + kb, 2 * t], limits[4 + kb, 2 * t + 1]

                @pl.when(jnp.logical_and(low <= q_high, high >= q_low))
                def _():
                    tile(kb, pl.multiple_of(t * (count // tiles), 128), count // tiles, True)

                return 0

            lax.fori_loop(0, tiles, half, 0)

        return 0

    lax.fori_loop(0, 4, key_block_step, 0)


def store_partial(out, row_max, total):
    def split(value, parts):
        pieces = []
        for _ in range(parts):
            piece = value.astype(bf16).astype(f32)
            pieces.append(piece)
            value = value - piece
        return pieces

    rows = split(total[80:81, :], 2) + split(row_max[...], 3)
    rows.append(jnp.zeros((3, out.shape[1]), f32))
    out[0:80, :] = total[0:80, :].astype(bf16)
    out[80:88, :] = jnp.concatenate(rows, axis=0).astype(bf16)


def copy_limits(limits, limits_s, sem):
    copy = pltpu.make_async_copy(limits, limits_s, sem)
    copy.start()
    copy.wait()


def attend_first_kernel(blocks, *refs):
    queries, key_values = refs[0:4], refs[4:8]
    outs = refs[8 : 8 + len(blocks)]
    held_k, held_v, limits, query, ids, limits_s, row_max, total, sem = refs[8 + len(blocks) :]
    count = queries[0].shape[1]
    for i in range(4):
        held_k[i] = key_values[i][0:80, :].T
        held_v[i] = key_values[i][80:168, :]
        ids[i : i + 1, :] = queries[i][80:88, :].astype(f32)[0:1, :]
        ids[4 + i : 5 + i, :] = key_values[i][160:168, :].astype(f32)[1:2, :]
    lane = lax.broadcasted_iota(jnp.int32, (8, 128), 1)
    table = jnp.zeros((8, 128), f32)
    for t in range(2):
        part = ids[:, t * (count // 2) : (t + 1) * (count // 2)]
        table = jnp.where(lane == 2 * t, jnp.min(part, axis=1, keepdims=True), table)
        table = jnp.where(lane == 2 * t + 1, jnp.max(part, axis=1, keepdims=True), table)
    limits[...] = table.astype(jnp.int32)
    copy_limits(limits, limits_s, sem)
    for i, block in enumerate(blocks):
        query[i] = queries[block][...]

    def one(i, unused):
        attend_block(query.at[i], held_k, held_v, limits_s, blocks[0] + i, row_max, total)
        for o in range(len(blocks)):

            @pl.when(i == o)
            def _():
                store_partial(outs[o], row_max, total)

        return 0

    lax.fori_loop(0, len(blocks), one, 0)


def attend_first(queries, key_values, blocks):
    count = queries[0].shape[1]
    return pl.pallas_call(
        functools.partial(attend_first_kernel, blocks),
        out_shape=[jax.ShapeDtypeStruct((88, count), bf16)] * len(blocks)
        + [
            jax.ShapeDtypeStruct((4, count, 80), bf16),
            jax.ShapeDtypeStruct((4, 88, count), bf16),
            jax.ShapeDtypeStruct((8, 128), jnp.int32),
        ],
        in_specs=[IN_VMEM] * 8,
        out_specs=[IN_VMEM] * (3 + len(blocks)),
        scratch_shapes=[
            pltpu.VMEM((len(blocks), 88, count), bf16),
            pltpu.VMEM((8, count), f32),
            pltpu.SMEM((8, 128), jnp.int32),
            pltpu.VMEM((1, count), f32),
            pltpu.VMEM((88, count), f32),
            pltpu.SemaphoreType.DMA,
        ],
        compiler_params=pltpu.CompilerParams(vmem_limit_bytes=16 << 20),
        name="attend_first",
    )(*queries, *key_values)


def attend_next_kernel(block, query, held_k, held_v, limits, out, limits_s, row_max, total, sem):
    copy_limits(limits, limits_s, sem)
    attend_block(query, held_k, held_v, limits_s, block, row_max, total)
    store_partial(out, row_max, total)


def attend_next(block, query, held_k, held_v, limits):
    count = query.shape[1]
    return pl.pallas_call(
        functools.partial(attend_next_kernel, block),
        out_shape=jax.ShapeDtypeStruct((88, count), bf16),
        in_specs=[IN_VMEM] * 4,
        out_specs=IN_VMEM,
        scratch_shapes=[
            pltpu.SMEM((8, 128), jnp.int32),
            pltpu.VMEM((1, count), f32),
            pltpu.VMEM((88, count), f32),
            pltpu.SemaphoreType.DMA,
        ],
        compiler_params=pltpu.CompilerParams(vmem_limit_bytes=12 << 20),
        name="attend_next",
    )(query, held_k, held_v, limits)


def combine_kernel(*refs):
    parts, out = refs[:4], refs[4]
    sums, maxima = [], []
    for part in parts:
        rows = part[80:88, :].astype(f32)
        sums.append(rows[0:1, :] + rows[1:2, :])
        maxima.append((rows[2:3, :] + rows[3:4, :]) + rows[4:5, :])
    top = functools.reduce(jnp.maximum, maxima)
    factors = [jnp.exp2((m - top) * EXP2_SCALE) for m in maxima]
    whole = functools.reduce(jnp.add, [w * s for w, s in zip(factors, sums)])
    inverse = 1.0 / whole
    mixed = functools.reduce(
        jnp.add, [part[0:80, :].astype(f32) * w for part, w in zip(parts, factors)]
    )
    out[...] = (mixed * inverse).astype(bf16)


def combine(parts):
    count = parts[0].shape[1]
    return pl.pallas_call(
        combine_kernel,
        out_shape=jax.ShapeDtypeStruct((80, count), bf16),
        in_specs=[IN_VMEM] * 4,
        out_specs=IN_VMEM,
        compiler_params=pltpu.CompilerParams(vmem_limit_bytes=6 << 20),
        name="combine",
    )(*parts)


def place_heads(heads, at, pieces, whole, sems):
    copies = []
    for piece in pieces:
        for i in range(piece.shape[0] // HDIM):
            row = pl.multiple_of(heads[at + len(copies)] * HDIM, 16)
            source = piece if piece.shape[0] == HDIM else piece.at[pl.ds(i * HDIM, HDIM), :]
            copy = pltpu.make_async_copy(source, whole.at[pl.ds(row, HDIM), :], sems.at[len(copies)])
            copy.start()
            copies.append(copy)
    return copies


def assemble_kernel(heads, *refs):
    pieces, whole, sems = refs[:-2], refs[-2], refs[-1]
    for copy in place_heads(heads, 16, pieces, whole, sems):
        copy.wait()


def assemble(heads, pieces):
    return pl.pallas_call(
        assemble_kernel,
        out_shape=jax.ShapeDtypeStruct((8 * HDIM, pieces[0].shape[1]), bf16),
        in_specs=[IN_SMEM] + [pl.BlockSpec(memory_space=pl.ANY)] * len(pieces),
        out_specs=IN_VMEM,
        scratch_shapes=[pltpu.SemaphoreType.DMA((8,))],
        compiler_params=pltpu.CompilerParams(vmem_limit_bytes=5 << 20),
        name="assemble",
    )(heads, *pieces)


def project_kernel(count, heads, *refs):
    pieces = refs[:10]
    halves, (gain, shift, proj, proj_bias, out, weight, attended, normed, sems) = refs[10:12], refs[12:]
    copies = place_heads(heads, 0, pieces, attended, sems)
    for i, half in enumerate(halves):
        rows = pl.ds(i * half.shape[0], half.shape[0])
        copies.append(pltpu.make_async_copy(half, weight.at[rows, :], sems.at[16 + i]))
        copies[-1].start()
    width = weight.shape[1]
    step = 512
    bias_column = jnp.broadcast_to(proj_bias[...], (8, proj.shape[0])).T[:, 0:1]
    for copy in copies:
        copy.wait()
    for b in range(count // step):
        turned = attended[:, b * step : (b + 1) * step].T
        rows = jnp.dot(turned, weight[...], preferred_element_type=f32).astype(bf16).astype(f32)
        rows = rows - jnp.sum(rows, axis=1, keepdims=True) * (1.0 / width)
        spread = jnp.sum(rows * rows, axis=1, keepdims=True) * (1.0 / width)
        rows = rows * lax.rsqrt(spread + EPSILON) * gain[...] + shift[...]
        for k in range(width // 128):
            normed[b, k] = rows[:, k * 128 : (k + 1) * 128]
        linear = jnp.zeros((proj.shape[0], step // 4), f32)
        for r in range(4):
            every_fourth = pl.ds(r, step // 4, stride=4)
            tokens = jnp.concatenate(
                [normed[b, k, every_fourth, :].astype(bf16) for k in range(width // 128)], axis=1
            )
            linear = linear + lax.dot_general(
                proj[:, r * width : (r + 1) * width],
                tokens,
                (((1,), (1,)), ((), ())),
                preferred_element_type=f32,
            )
        linear = linear + bias_column
        active = 0.5 * linear * (1.0 + lax.erf(linear * (0.5**0.5)))
        out[:, b * (step // 4) : (b + 1) * (step // 4)] = active.astype(bf16)


def project(heads, pieces, halves, gain, shift, proj, proj_bias):
    count = pieces[0].shape[1]
    depth, width = 2 * halves[0].shape[0], halves[0].shape[1]
    return pl.pallas_call(
        functools.partial(project_kernel, count),
        out_shape=jax.ShapeDtypeStruct((proj.shape[0], count // 4), bf16),
        in_specs=[IN_SMEM] + [pl.BlockSpec(memory_space=pl.ANY)] * 12 + [IN_VMEM] * 4,
        out_specs=IN_VMEM,
        scratch_shapes=[
            pltpu.VMEM((depth, width), bf16),
            pltpu.VMEM((depth, count), bf16),
            pltpu.VMEM((count // 512, width // 128, 512, 128), f32),
            pltpu.SemaphoreType.DMA((18,)),
        ],
        compiler_params=pltpu.CompilerParams(vmem_limit_bytes=30 << 20),
        name="project",
    )(heads, *pieces, *halves, gain, shift, proj, proj_bias)


def head_order():
    table = []
    for x in range(4):
        for c in range(2):
            for t in range(2):

                def slot(a, d, b):
                    return (d != c) * 8 + a % 4 * 2 + b

                row = [slot(x, c, t), slot(x, 1 - c, t)]
                for d in (c, 1 - c):
                    side = x + (3, 1)[d]
                    cross = (x + 2, t) if d == 0 else (x, 1 - t)
                    row += [slot(side, d, t), slot(side, 1 - d, t)]
                    row += [slot(cross[0], d, cross[1]), slot(cross[0], 1 - d, cross[1])]
                    row += [slot(side, d, 1 - t), slot(side, 1 - d, 1 - t)]
                    row += [slot(x + 2, d, 1 - t)]
                for a in (x, x + 3, x + 1, x + 2):
                    row += [slot(a, c, t), slot(a, c, 1 - t)]
                table.append(row)
    return table


def on_device(
    queries, keys, values, segment_ids, out_weight, norm_gain, norm_bias, proj_weight, proj_bias
):
    blocks = lax.axis_size("blk")
    query_block, key_block = pack(queries.T, keys.T, values.T, segment_ids[None, :])

    sections = lax.axis_size("section")

    def swap(block, mask):
        if mask == 0:
            return block
        perm = []
        for i in range(blocks):
            for section in range(sections):
                turn = section % 2
                y, z = i // 8 ^ mask >> 3, ((i % 8 - turn) % 8 ^ mask & 7) + turn
                perm.append((i * sections + section, (y * 8 + z % 8) * sections + section))
        return lax.ppermute(block, ("blk", "section"), perm)

    def send(block, to):
        perm = []
        for x in range(4):
            for c in range(2):
                for t in range(2):
                    a, b, d = to(x, c, t)
                    perm.append(((x * 2 + c) * 2 + t, (a % 4 * 2 + b) * 2 + d))
        return lax.ppermute(block, GROUP, perm)

    far = send(out_weight, lambda x, c, t: (x, c, 1 - t))
    both = jnp.concatenate([out_weight, far], axis=0)
    me = lax.axis_index("section") * 2 + lax.axis_index("tp")
    heads = jnp.asarray(head_order(), jnp.int32)[me]

    def across(x, c, t):
        return x, 1 - c, t

    key_blocks = [swap(key_block, mask) for mask in KEY_PARTNERS]
    query_blocks = [swap(query_block, mask) for mask in QUERY_PARTNERS]
    both, query_blocks, key_blocks = lax.optimization_barrier((both, query_blocks, key_blocks))
    weights = [both] + [send(both, lambda x, c, t, d=d: (x + d, c, t)) for d in (1, 3, 2)]
    *partial, held_k, held_v, limits = attend_first(query_blocks, key_blocks, (1, 2))
    returned = [swap(part, mask) for part, mask in zip(partial, QUERY_PARTNERS[1:3])]
    third = attend_next(3, query_blocks[3], held_k, held_v, limits)
    returned.append(swap(third, QUERY_PARTNERS[3]))
    own_query, third = lax.optimization_barrier((query_blocks[0], third))
    returned.append(attend_next(0, own_query, held_k, held_v, limits))
    weights, returned[3] = lax.optimization_barrier((weights, returned[3]))
    half = assemble(heads, weights)
    returned, half = lax.optimization_barrier((returned, half))
    attended = combine(returned)
    halves = [half, send(half, across)]

    def along(x, c, t):
        return x + (1, -1)[c], c, t

    def along_far(x, c, t):
        return x + (1, -1)[c], c, 1 - t

    def opposite(x, c, t):
        return (x + 2, c, t) if c == 0 else (x, c, 1 - t)

    def opposite_far(x, c, t):
        return x + 2, c, 1 - t

    sibling = send(attended, across)
    pair = jnp.concatenate([attended, sibling], axis=0)
    received = [send(pair, along), send(pair, opposite), send(pair, along_far)]
    received.append(send(attended, opposite_far))
    forwarded = [send(block, across) for block in received]
    pieces = [attended, sibling] + received + forwarded
    projected = project(
        heads,
        pieces,
        halves,
        norm_gain[None, :],
        norm_bias[None, :],
        proj_weight.T,
        proj_bias[None, :],
    )
    return projected.T


def solution(mesh):
    placed = (
        P("blk", GROUP),
        P("blk", GROUP),
        P("blk", GROUP),
        P("blk"),
        P(GROUP, None),
        P(),
        P(),
        P(None, GROUP),
        P(GROUP),
    )
    return jax.shard_map(
        on_device,
        mesh=mesh,
        in_specs=placed,
        out_specs=P("blk", GROUP),
        check_vma=False,
    )
```

```python
import functools

import jax
import jax.numpy as jnp
from jax import lax
from jax.experimental import pallas as pl
from jax.experimental.pallas import tpu as pltpu
from jax.sharding import PartitionSpec as P

HDIM = 80
EPSILON = 1e-06
EXP2_SCALE = 1.4426950408889634 * HDIM ** (-0.5)
MASKED = -1e30
NO_MAX = -1e20
MOST_EXCESS = 60.0 / EXP2_SCALE
KEY_PARTNERS = (0, 1, 8, 9)
QUERY_PARTNERS = (0, 4, 10, 14)
f32, bf16 = jnp.float32, jnp.bfloat16
GROUP = ("section", "tp")
IN_VMEM = pl.BlockSpec(memory_space=pltpu.VMEM)
IN_SMEM = pl.BlockSpec(memory_space=pltpu.SMEM)


def pack_kernel(queries, keys, values, ids, query_block, key_block, held_ids, sems):
    count = queries.shape[1]
    moves = [
        (ids, held_ids),
        (queries, query_block.at[0:80, :]),
        (keys, key_block.at[0:80, :]),
        (values, key_block.at[80:160, :]),
    ]
    copies = [pltpu.make_async_copy(*move, sems.at[i]) for i, move in enumerate(moves)]
    for copy in copies:
        copy.start()
    copies[0].wait()
    id_row = held_ids[...].astype(f32)
    zeros = jnp.zeros((6, count), f32)
    query_block[80:88, :] = jnp.concatenate([id_row, id_row, zeros], axis=0).astype(bf16)
    key_block[160:168, :] = jnp.concatenate([jnp.ones_like(id_row), id_row, zeros], axis=0).astype(bf16)
    for copy in copies[1:]:
        copy.wait()


def pack(queries, keys, values, ids):
    count = queries.shape[1]
    return pl.pallas_call(
        pack_kernel,
        out_shape=[
            jax.ShapeDtypeStruct((88, count), bf16),
            jax.ShapeDtypeStruct((168, count), bf16),
        ],
        in_specs=[pl.BlockSpec(memory_space=pltpu.HBM)] * 4,
        out_specs=[IN_VMEM] * 2,
        scratch_shapes=[pltpu.VMEM((1, count), jnp.int32), pltpu.SemaphoreType.DMA((4,))],
        compiler_params=pltpu.CompilerParams(vmem_limit_bytes=4 << 20),
        name="pack",
    )(*(pltpu.with_memory_space_constraint(x, pltpu.HBM) for x in (queries, keys, values, ids)))


def attend_block(query, held_k, held_v, limits, which, row_max, total, excess):
    count = query.shape[1]
    tiles, sub = 2, 256
    q_low, q_high = limits[which, 0], limits[which, 3]

    def tile(kb, start, tile_keys, masked, raising):
        rows = pl.ds(start, tile_keys)
        key_tile = held_k[kb, rows, :]
        value_tile = held_v[kb, :, rows]
        if masked:
            key_ids = jnp.broadcast_to(value_tile[80:88, :].T.astype(f32)[:, 1:2], (tile_keys, sub))

        def score(j):
            columns = slice(j * sub, (j + 1) * sub)
            found = jnp.dot(key_tile, query[0:80, columns], preferred_element_type=f32)
            if masked:
                query_ids = query[80:88, columns].astype(f32)[0:1, :]
                found = jnp.where(key_ids == query_ids, found, MASKED)
            return found

        scores = score(0)
        for j in range(count // sub):
            following = score(j + 1) if (j + 1) * sub < count else None
            columns = slice(j * sub, (j + 1) * sub)
            old = row_max[:, columns]
            if raising:
                new = jnp.maximum(old, jnp.max(scores, axis=0, keepdims=True))
                weights = jnp.exp2((scores - new) * EXP2_SCALE).astype(bf16)
                rescale = jnp.exp2((old - new) * EXP2_SCALE)
                total[:, columns] = total[:, columns] * rescale + jnp.dot(
                    value_tile, weights, preferred_element_type=f32
                )
                row_max[:, columns] = new
            else:
                weights = jnp.exp2((scores - old) * EXP2_SCALE).astype(bf16)
                total[:, columns] = total[:, columns] + jnp.dot(
                    value_tile, weights, preferred_element_type=f32
                )
                above = jnp.max(scores, axis=0, keepdims=True) - old
                excess[:, columns] = jnp.maximum(excess[:, columns], above)
            scores = following

    def every_key_block(keep_shift):
        row_max[...] = jnp.full_like(row_max, NO_MAX)
        total[...] = jnp.zeros_like(total)
        excess[...] = jnp.zeros_like(excess)

        def key_block_step(kb, started):
            low, high = limits[4 + kb, 0], limits[4 + kb, 3]
            whole = jnp.logical_and(jnp.logical_and(low == high, q_low == q_high), low == q_low)
            still = jnp.logical_and(jnp.logical_and(whole, started > 0), keep_shift)

            @pl.when(still)
            def _():
                tile(kb, 0, count, False, False)

            @pl.when(jnp.logical_and(whole, jnp.logical_not(still)))
            def _():
                tile(kb, 0, count, False, True)

            @pl.when(jnp.logical_not(whole))
            def _():
                def half(t, unused):
                    low, high = limits[4 + kb, 2 * t], limits[4 + kb, 2 * t + 1]

                    @pl.when(jnp.logical_and(low <= q_high, high >= q_low))
                    def _():
                        tile(kb, pl.multiple_of(t * (count // tiles), 128), count // tiles, True, True)

                    return 0

                lax.fori_loop(0, tiles, half, 0)

            return jnp.maximum(started, whole.astype(jnp.int32))

        lax.fori_loop(0, 4, key_block_step, 0)

    def attempt(tried, unused):
        @pl.when(jnp.logical_or(tried == 0, jnp.max(excess[...]) > MOST_EXCESS))
        def _():
            every_key_block(tried == 0)

        return 0

    lax.fori_loop(0, 2, attempt, 0)


def store_partial(out, row_max, total):
    def split(value, parts):
        pieces = []
        for _ in range(parts):
            piece = value.astype(bf16).astype(f32)
            pieces.append(piece)
            value = value - piece
        return pieces

    rows = split(total[80:81, :], 2) + split(row_max[...], 3)
    rows.append(jnp.zeros((3, out.shape[1]), f32))
    out[0:80, :] = total[0:80, :].astype(bf16)
    out[80:88, :] = jnp.concatenate(rows, axis=0).astype(bf16)


def copy_limits(limits, limits_s, sem):
    copy = pltpu.make_async_copy(limits, limits_s, sem)
    copy.start()
    copy.wait()


def attend_first_kernel(blocks, *refs):
    queries, key_values = refs[0:4], refs[4:8]
    outs = refs[8 : 8 + len(blocks)]
    (held_k, held_v, limits, query, ids, limits_s, row_max, total, excess, sem) = refs[8 + len(blocks) :]
    count = queries[0].shape[1]
    for i in range(4):
        held_k[i] = key_values[i][0:80, :].T
        held_v[i] = key_values[i][80:168, :]
        ids[i : i + 1, :] = queries[i][80:88, :].astype(f32)[0:1, :]
        ids[4 + i : 5 + i, :] = key_values[i][160:168, :].astype(f32)[1:2, :]
    lane = lax.broadcasted_iota(jnp.int32, (8, 128), 1)
    table = jnp.zeros((8, 128), f32)
    for t in range(2):
        part = ids[:, t * (count // 2) : (t + 1) * (count // 2)]
        table = jnp.where(lane == 2 * t, jnp.min(part, axis=1, keepdims=True), table)
        table = jnp.where(lane == 2 * t + 1, jnp.max(part, axis=1, keepdims=True), table)
    limits[...] = table.astype(jnp.int32)
    copy_limits(limits, limits_s, sem)
    for i, block in enumerate(blocks):
        query[i] = queries[block][...]

    def one(i, unused):
        attend_block(query.at[i], held_k, held_v, limits_s, blocks[0] + i, row_max, total, excess)
        for o in range(len(blocks)):

            @pl.when(i == o)
            def _():
                store_partial(outs[o], row_max, total)

        return 0

    lax.fori_loop(0, len(blocks), one, 0)


def attend_first(queries, key_values, blocks):
    count = queries[0].shape[1]
    return pl.pallas_call(
        functools.partial(attend_first_kernel, blocks),
        out_shape=[jax.ShapeDtypeStruct((88, count), bf16)] * len(blocks)
        + [
            jax.ShapeDtypeStruct((4, count, 80), bf16),
            jax.ShapeDtypeStruct((4, 88, count), bf16),
            jax.ShapeDtypeStruct((8, 128), jnp.int32),
        ],
        in_specs=[IN_VMEM] * 8,
        out_specs=[IN_VMEM] * (3 + len(blocks)),
        scratch_shapes=[
            pltpu.VMEM((len(blocks), 88, count), bf16),
            pltpu.VMEM((8, count), f32),
            pltpu.SMEM((8, 128), jnp.int32),
            pltpu.VMEM((1, count), f32),
            pltpu.VMEM((88, count), f32),
            pltpu.VMEM((1, count), f32),
            pltpu.SemaphoreType.DMA,
        ],
        compiler_params=pltpu.CompilerParams(vmem_limit_bytes=16 << 20),
        name="attend_first",
    )(*queries, *key_values)


def attend_next_kernel(
    block, query, held_k, held_v, limits, out, limits_s, row_max, total, excess, sem
):
    copy_limits(limits, limits_s, sem)
    attend_block(query, held_k, held_v, limits_s, block, row_max, total, excess)
    store_partial(out, row_max, total)


def attend_next(block, query, held_k, held_v, limits):
    count = query.shape[1]
    return pl.pallas_call(
        functools.partial(attend_next_kernel, block),
        out_shape=jax.ShapeDtypeStruct((88, count), bf16),
        in_specs=[IN_VMEM] * 4,
        out_specs=IN_VMEM,
        scratch_shapes=[
            pltpu.SMEM((8, 128), jnp.int32),
            pltpu.VMEM((1, count), f32),
            pltpu.VMEM((88, count), f32),
            pltpu.VMEM((1, count), f32),
            pltpu.SemaphoreType.DMA,
        ],
        compiler_params=pltpu.CompilerParams(vmem_limit_bytes=12 << 20),
        name="attend_next",
    )(query, held_k, held_v, limits)


def combine_kernel(*refs):
    parts, out = refs[:4], refs[4]
    sums, maxima = [], []
    for part in parts:
        rows = part[80:88, :].astype(f32)
        sums.append(rows[0:1, :] + rows[1:2, :])
        maxima.append((rows[2:3, :] + rows[3:4, :]) + rows[4:5, :])
    top = functools.reduce(jnp.maximum, maxima)
    factors = [jnp.exp2((m - top) * EXP2_SCALE) for m in maxima]
    whole = functools.reduce(jnp.add, [w * s for w, s in zip(factors, sums)])
    inverse = 1.0 / whole
    mixed = functools.reduce(
        jnp.add, [part[0:80, :].astype(f32) * w for part, w in zip(parts, factors)]
    )
    out[...] = (mixed * inverse).astype(bf16)


def combine(parts):
    count = parts[0].shape[1]
    return pl.pallas_call(
        combine_kernel,
        out_shape=jax.ShapeDtypeStruct((80, count), bf16),
        in_specs=[IN_VMEM] * 4,
        out_specs=IN_VMEM,
        compiler_params=pltpu.CompilerParams(vmem_limit_bytes=6 << 20),
        name="combine",
    )(*parts)


def place_heads(heads, at, pieces, whole, sems):
    copies = []
    for piece in pieces:
        for i in range(piece.shape[0] // HDIM):
            row = pl.multiple_of(heads[at + len(copies)] * HDIM, 16)
            source = piece if piece.shape[0] == HDIM else piece.at[pl.ds(i * HDIM, HDIM), :]
            copy = pltpu.make_async_copy(source, whole.at[pl.ds(row, HDIM), :], sems.at[len(copies)])
            copy.start()
            copies.append(copy)
    return copies


def assemble_kernel(heads, *refs):
    pieces, whole, sems = refs[:-2], refs[-2], refs[-1]
    for copy in place_heads(heads, 16, pieces, whole, sems):
        copy.wait()


def assemble(heads, pieces):
    return pl.pallas_call(
        assemble_kernel,
        out_shape=jax.ShapeDtypeStruct((8 * HDIM, pieces[0].shape[1]), bf16),
        in_specs=[IN_SMEM] + [pl.BlockSpec(memory_space=pl.ANY)] * len(pieces),
        out_specs=IN_VMEM,
        scratch_shapes=[pltpu.SemaphoreType.DMA((8,))],
        compiler_params=pltpu.CompilerParams(vmem_limit_bytes=5 << 20),
        name="assemble",
    )(heads, *pieces)


def join_kernel(*refs):
    halves, whole, sems = refs[:-2], refs[-2], refs[-1]
    rows = halves[0].shape[0]
    copies = [
        pltpu.make_async_copy(half, whole.at[pl.ds(i * rows, rows), :], sems.at[i])
        for i, half in enumerate(halves)
    ]
    for copy in copies:
        copy.start()
    for copy in copies:
        copy.wait()


def join(halves):
    rows, width = halves[0].shape
    return pl.pallas_call(
        join_kernel,
        out_shape=jax.ShapeDtypeStruct((len(halves) * rows, width), bf16),
        in_specs=[pl.BlockSpec(memory_space=pl.ANY)] * len(halves),
        out_specs=IN_VMEM,
        scratch_shapes=[pltpu.SemaphoreType.DMA((len(halves),))],
        compiler_params=pltpu.CompilerParams(vmem_limit_bytes=5 << 20),
        name="join",
    )(*halves)


def project_kernel(count, heads, *refs):
    pieces = refs[:10]
    (weight, gain, shift, proj, proj_bias, out, attended, normed, sems) = refs[10:]
    copies = place_heads(heads, 0, pieces, attended, sems)
    width = weight.shape[1]
    step = 512
    bias_column = jnp.broadcast_to(proj_bias[...], (8, proj.shape[0])).T[:, 0:1]
    for copy in copies:
        copy.wait()
    for b in range(count // step):
        turned = attended[:, b * step : (b + 1) * step].T
        rows = jnp.dot(turned, weight[...], preferred_element_type=f32).astype(bf16).astype(f32)
        rows = rows - jnp.sum(rows, axis=1, keepdims=True) * (1.0 / width)
        spread = jnp.sum(rows * rows, axis=1, keepdims=True) * (1.0 / width)
        rows = rows * lax.rsqrt(spread + EPSILON) * gain[...] + shift[...]
        for k in range(width // 128):
            normed[b, k] = rows[:, k * 128 : (k + 1) * 128]
        linear = jnp.zeros((proj.shape[0], step // 4), f32)
        for r in range(4):
            every_fourth = pl.ds(r, step // 4, stride=4)
            tokens = jnp.concatenate(
                [normed[b, k, every_fourth, :].astype(bf16) for k in range(width // 128)], axis=1
            )
            linear = linear + lax.dot_general(
                proj[:, r * width : (r + 1) * width],
                tokens,
                (((1,), (1,)), ((), ())),
                preferred_element_type=f32,
            )
        linear = linear + bias_column
        active = 0.5 * linear * (1.0 + lax.erf(linear * (0.5**0.5)))
        out[:, b * (step // 4) : (b + 1) * (step // 4)] = active.astype(bf16)


def project(heads, pieces, weight, gain, shift, proj, proj_bias):
    count = pieces[0].shape[1]
    depth, width = weight.shape
    return pl.pallas_call(
        functools.partial(project_kernel, count),
        out_shape=jax.ShapeDtypeStruct((proj.shape[0], count // 4), bf16),
        in_specs=[IN_SMEM] + [pl.BlockSpec(memory_space=pl.ANY)] * 10 + [IN_VMEM] * 5,
        out_specs=IN_VMEM,
        scratch_shapes=[
            pltpu.VMEM((depth, count), bf16),
            pltpu.VMEM((count // 512, width // 128, 512, 128), f32),
            pltpu.SemaphoreType.DMA((16,)),
        ],
        compiler_params=pltpu.CompilerParams(vmem_limit_bytes=30 << 20),
        name="project",
    )(heads, *pieces, weight, gain, shift, proj, proj_bias)


def head_order():
    table = []
    for x in range(4):
        for c in range(2):
            for t in range(2):

                def slot(a, d, b):
                    return (d != c) * 8 + a % 4 * 2 + b

                row = [slot(x, c, t), slot(x, 1 - c, t)]
                for d in (c, 1 - c):
                    side = x + (3, 1)[d]
                    cross = (x + 2, t) if d == 0 else (x, 1 - t)
                    row += [slot(side, d, t), slot(side, 1 - d, t)]
                    row += [slot(cross[0], d, cross[1]), slot(cross[0], 1 - d, cross[1])]
                    row += [slot(side, d, 1 - t), slot(side, 1 - d, 1 - t)]
                    row += [slot(x + 2, d, 1 - t)]
                for a in (x, x + 3, x + 1, x + 2):
                    row += [slot(a, c, t), slot(a, c, 1 - t)]
                table.append(row)
    return table


def on_device(
    queries, keys, values, segment_ids, out_weight, norm_gain, norm_bias, proj_weight, proj_bias
):
    blocks = lax.axis_size("blk")
    query_block, key_block = pack(queries.T, keys.T, values.T, segment_ids[None, :])

    sections = lax.axis_size("section")

    def swap(block, mask):
        if mask == 0:
            return block
        perm = []
        for i in range(blocks):
            for section in range(sections):
                turn = section % 2
                y, z = i // 8 ^ mask >> 3, ((i % 8 - turn) % 8 ^ mask & 7) + turn
                perm.append((i * sections + section, (y * 8 + z % 8) * sections + section))
        return lax.ppermute(block, ("blk", "section"), perm)

    def send(block, to):
        perm = []
        for x in range(4):
            for c in range(2):
                for t in range(2):
                    a, b, d = to(x, c, t)
                    perm.append(((x * 2 + c) * 2 + t, (a % 4 * 2 + b) * 2 + d))
        return lax.ppermute(block, GROUP, perm)

    far = send(out_weight, lambda x, c, t: (x, c, 1 - t))
    me = lax.axis_index("section") * 2 + lax.axis_index("tp")
    heads = jnp.asarray(head_order(), jnp.int32)[me]

    def across(x, c, t):
        return x, 1 - c, t

    key_blocks = [swap(key_block, mask) for mask in KEY_PARTNERS]
    query_blocks = [swap(query_block, mask) for mask in QUERY_PARTNERS]
    both = jnp.concatenate([out_weight, far], axis=0)
    both, query_blocks, key_blocks = lax.optimization_barrier((both, query_blocks, key_blocks))
    weights = [both] + [send(both, lambda x, c, t, d=d: (x + d, c, t)) for d in (1, 3, 2)]
    *partial, held_k, held_v, limits = attend_first(query_blocks, key_blocks, (1, 2, 3))
    returned = [swap(part, mask) for part, mask in zip(partial, QUERY_PARTNERS[1:])]
    own_query, partial = lax.optimization_barrier((query_blocks[0], partial))
    returned.append(attend_next(0, own_query, held_k, held_v, limits))
    weights, returned[3] = lax.optimization_barrier((weights, returned[3]))
    half = assemble(heads, weights)
    returned, half = lax.optimization_barrier((returned, half))
    other_half = send(half, across)
    attended = combine(returned)

    def along(x, c, t):
        return x + (1, -1)[c], c, t

    def along_far(x, c, t):
        return x + (1, -1)[c], c, 1 - t

    def opposite(x, c, t):
        return (x + 2, c, t) if c == 0 else (x, c, 1 - t)

    def opposite_far(x, c, t):
        return x + 2, c, 1 - t

    sibling = send(attended, across)
    pair = jnp.concatenate([attended, sibling], axis=0)
    received = [send(pair, along), send(pair, opposite), send(pair, along_far)]
    received.append(send(attended, opposite_far))
    weight, received[-1] = lax.optimization_barrier((join([half, other_half]), received[-1]))
    forwarded = [send(block, across) for block in received]
    pieces = [attended, sibling] + received + forwarded
    projected = project(
        heads,
        pieces,
        weight,
        norm_gain[None, :],
        norm_bias[None, :],
        proj_weight.T,
        proj_bias[None, :],
    )
    return projected.T


def solution(mesh):
    placed = (
        P("blk", GROUP),
        P("blk", GROUP),
        P("blk", GROUP),
        P("blk"),
        P(GROUP, None),
        P(),
        P(),
        P(None, GROUP),
        P(GROUP),
    )
    return jax.shard_map(
        on_device,
        mesh=mesh,
        in_specs=placed,
        out_specs=P("blk", GROUP),
        check_vma=False,
    )
```

```python
import functools

import jax
import jax.numpy as jnp
from jax import lax
from jax.experimental import pallas as pl
from jax.experimental.pallas import tpu as pltpu
from jax.sharding import PartitionSpec as P

HDIM = 80
EPSILON = 1e-06
EXP2_SCALE = 1.4426950408889634 * HDIM ** (-0.5)
MASKED = -1e30
NO_MAX = -1e20
MOST_EXCESS = 60.0 / EXP2_SCALE
KEY_PARTNERS = (0, 1, 8, 9)
QUERY_PARTNERS = (0, 4, 10, 14)
f32, bf16 = jnp.float32, jnp.bfloat16
GROUP = ("section", "tp")
IN_VMEM = pl.BlockSpec(memory_space=pltpu.VMEM)
IN_SMEM = pl.BlockSpec(memory_space=pltpu.SMEM)


def pack_kernel(queries, keys, values, ids, query_block, key_block, held_ids, sems):
    count = queries.shape[1]
    moves = [
        (ids, held_ids),
        (queries, query_block.at[0:80, :]),
        (keys, key_block.at[0:80, :]),
        (values, key_block.at[80:160, :]),
    ]
    copies = [pltpu.make_async_copy(*move, sems.at[i]) for i, move in enumerate(moves)]
    for copy in copies:
        copy.start()
    copies[0].wait()
    id_row = held_ids[...].astype(f32)
    zeros = jnp.zeros((6, count), f32)
    query_block[80:88, :] = jnp.concatenate([id_row, id_row, zeros], axis=0).astype(bf16)
    key_block[160:168, :] = jnp.concatenate([jnp.ones_like(id_row), id_row, zeros], axis=0).astype(bf16)
    for copy in copies[1:]:
        copy.wait()


def pack(queries, keys, values, ids):
    count = queries.shape[1]
    return pl.pallas_call(
        pack_kernel,
        out_shape=[
            jax.ShapeDtypeStruct((88, count), bf16),
            jax.ShapeDtypeStruct((168, count), bf16),
        ],
        in_specs=[pl.BlockSpec(memory_space=pltpu.HBM)] * 4,
        out_specs=[IN_VMEM] * 2,
        scratch_shapes=[pltpu.VMEM((1, count), jnp.int32), pltpu.SemaphoreType.DMA((4,))],
        compiler_params=pltpu.CompilerParams(vmem_limit_bytes=4 << 20),
        name="pack",
    )(*(pltpu.with_memory_space_constraint(x, pltpu.HBM) for x in (queries, keys, values, ids)))


def attend_block(query, held_k, held_v, limits, which, row_max, total, excess):
    count = query.shape[1]
    tiles, sub = 2, 256
    q_low, q_high = limits[which, 0], limits[which, 3]

    def tile(kb, start, tile_keys, masked, raising):
        rows = pl.ds(start, tile_keys)
        key_tile = held_k[kb, rows, :]
        value_tile = held_v[kb, :, rows]
        if masked:
            key_ids = jnp.broadcast_to(value_tile[80:88, :].T.astype(f32)[:, 1:2], (tile_keys, sub))

        def score(j):
            columns = slice(j * sub, (j + 1) * sub)
            found = jnp.dot(key_tile, query[0:80, columns], preferred_element_type=f32)
            if masked:
                query_ids = query[80:88, columns].astype(f32)[0:1, :]
                found = jnp.where(key_ids == query_ids, found, MASKED)
            return found

        scores = score(0)
        for j in range(count // sub):
            following = score(j + 1) if (j + 1) * sub < count else None
            columns = slice(j * sub, (j + 1) * sub)
            old = row_max[:, columns]
            if raising:
                new = jnp.maximum(old, jnp.max(scores, axis=0, keepdims=True))
                weights = jnp.exp2((scores - new) * EXP2_SCALE).astype(bf16)
                rescale = jnp.exp2((old - new) * EXP2_SCALE)
                total[:, columns] = total[:, columns] * rescale + jnp.dot(
                    value_tile, weights, preferred_element_type=f32
                )
                row_max[:, columns] = new
            else:
                weights = jnp.exp2((scores - old) * EXP2_SCALE).astype(bf16)
                total[:, columns] = total[:, columns] + jnp.dot(
                    value_tile, weights, preferred_element_type=f32
                )
                above = jnp.max(scores, axis=0, keepdims=True) - old
                excess[:, columns] = jnp.maximum(excess[:, columns], above)
            scores = following

    def every_key_block(keep_shift):
        row_max[...] = jnp.full_like(row_max, NO_MAX)
        total[...] = jnp.zeros_like(total)
        excess[...] = jnp.zeros_like(excess)

        def key_block_step(kb, started):
            low, high = limits[4 + kb, 0], limits[4 + kb, 3]
            live = jnp.logical_and(low <= q_high, high >= q_low)
            pure = q_low == q_high
            still = jnp.logical_and(
                jnp.logical_and(pure, jnp.logical_and(low == high, low == q_low)), keep_shift
            )

            @pl.when(jnp.logical_and(still, started == 0))
            def _():
                for j in range(count // sub):
                    columns = slice(j * sub, (j + 1) * sub)
                    found = jnp.dot(held_k[kb, 0:128, :], query[0:80, columns], preferred_element_type=f32)
                    row_max[:, columns] = jnp.max(found, axis=0, keepdims=True)

            @pl.when(still)
            def _():
                tile(kb, 0, count, False, False)

            @pl.when(jnp.logical_and(live, jnp.logical_not(still)))
            def _():
                def half(t, unused):
                    low, high = limits[4 + kb, 2 * t], limits[4 + kb, 2 * t + 1]

                    @pl.when(jnp.logical_and(low <= q_high, high >= q_low))
                    def _():
                        tile(kb, pl.multiple_of(t * (count // tiles), 128), count // tiles, True, True)

                    return 0

                lax.fori_loop(0, tiles, half, 0)

            return jnp.maximum(started, live.astype(jnp.int32))

        lax.fori_loop(0, 4, key_block_step, 0)

    def attempt(tried, unused):
        @pl.when(jnp.logical_or(tried == 0, jnp.max(excess[...]) > MOST_EXCESS))
        def _():
            every_key_block(tried == 0)

        return 0

    lax.fori_loop(0, 2, attempt, 0)


def store_partial(out, row_max, total):
    def split(value, parts):
        pieces = []
        for _ in range(parts):
            piece = value.astype(bf16).astype(f32)
            pieces.append(piece)
            value = value - piece
        return pieces

    rows = split(total[80:81, :], 2) + split(row_max[...], 3)
    rows.append(jnp.zeros((3, out.shape[1]), f32))
    out[0:80, :] = total[0:80, :].astype(bf16)
    out[80:88, :] = jnp.concatenate(rows, axis=0).astype(bf16)


def find_limits(ids, limits, limits_s, sem):
    count = ids.shape[1]
    lane = lax.broadcasted_iota(jnp.int32, (8, 128), 1)
    table = jnp.zeros((8, 128), f32)
    for t in range(2):
        part = ids[:, t * (count // 2) : (t + 1) * (count // 2)]
        table = jnp.where(lane == 2 * t, jnp.min(part, axis=1, keepdims=True), table)
        table = jnp.where(lane == 2 * t + 1, jnp.max(part, axis=1, keepdims=True), table)
    limits[...] = table.astype(jnp.int32)
    copy = pltpu.make_async_copy(limits, limits_s, sem)
    copy.start()
    copy.wait()


def attend_kernel(blocks, first, *refs):
    queries, refs = refs[:blocks], refs[blocks:]
    if first:
        key_values, refs = refs[:4], refs[4:]
    else:
        (held_k, held_v), refs = refs[:2], refs[2:]
    outs, refs = refs[:blocks], refs[blocks:]
    if first:
        (held_k, held_v), refs = refs[:2], refs[2:]
    query, ids, limits, limits_s, row_max, total, excess, sem = refs
    ids[...] = jnp.zeros_like(ids)
    for i in range(4):
        if first:
            held_k[i] = key_values[i][0:80, :].T
            held_v[i] = key_values[i][80:168, :]
        ids[4 + i : 5 + i, :] = held_v[i, 80:88, :].astype(f32)[1:2, :]
    for i in range(blocks):
        query[i] = queries[i][...]
        ids[i : i + 1, :] = queries[i][80:88, :].astype(f32)[0:1, :]
    find_limits(ids, limits, limits_s, sem)

    def one(i, unused):
        attend_block(query.at[i], held_k, held_v, limits_s, i, row_max, total, excess)
        for o in range(blocks):

            @pl.when(i == o)
            def _():
                store_partial(outs[o], row_max, total)

        return 0

    lax.fori_loop(0, blocks, one, 0)


def attend(queries, key_values, held=None):
    count = queries[0].shape[1]
    first = held is None
    shapes = [jax.ShapeDtypeStruct((88, count), bf16)] * len(queries)
    if first:
        shapes.append(jax.ShapeDtypeStruct((4, count, 80), bf16))
        shapes.append(jax.ShapeDtypeStruct((4, 88, count), bf16))
    operands = list(queries) + list(key_values if first else held)
    out = pl.pallas_call(
        functools.partial(attend_kernel, len(queries), first),
        out_shape=shapes,
        in_specs=[IN_VMEM] * len(operands),
        out_specs=[IN_VMEM] * len(shapes),
        scratch_shapes=[
            pltpu.VMEM((len(queries), 88, count), bf16),
            pltpu.VMEM((8, count), f32),
            pltpu.VMEM((8, 128), jnp.int32),
            pltpu.SMEM((8, 128), jnp.int32),
            pltpu.VMEM((1, count), f32),
            pltpu.VMEM((88, count), f32),
            pltpu.VMEM((1, count), f32),
            pltpu.SemaphoreType.DMA,
        ],
        compiler_params=pltpu.CompilerParams(vmem_limit_bytes=16 << 20),
        name="attend_first" if first else "attend_next",
    )(*operands)
    return list(out[: len(queries)]), list(out[len(queries) :])


def combine_kernel(*refs):
    parts, out = refs[:4], refs[4]
    sums, maxima = [], []
    for part in parts:
        rows = part[80:88, :].astype(f32)
        sums.append(rows[0:1, :] + rows[1:2, :])
        maxima.append((rows[2:3, :] + rows[3:4, :]) + rows[4:5, :])
    top = functools.reduce(jnp.maximum, maxima)
    factors = [jnp.exp2((m - top) * EXP2_SCALE) for m in maxima]
    whole = functools.reduce(jnp.add, [w * s for w, s in zip(factors, sums)])
    inverse = 1.0 / whole
    mixed = functools.reduce(
        jnp.add, [part[0:80, :].astype(f32) * w for part, w in zip(parts, factors)]
    )
    out[...] = (mixed * inverse).astype(bf16)


def combine(parts):
    count = parts[0].shape[1]
    return pl.pallas_call(
        combine_kernel,
        out_shape=jax.ShapeDtypeStruct((80, count), bf16),
        in_specs=[IN_VMEM] * 4,
        out_specs=IN_VMEM,
        compiler_params=pltpu.CompilerParams(vmem_limit_bytes=6 << 20),
        name="combine",
    )(*parts)


def place_heads(heads, at, pieces, whole, sems):
    copies = []
    for piece in pieces:
        for i in range(piece.shape[0] // HDIM):
            row = pl.multiple_of(heads[at + len(copies)] * HDIM, 16)
            source = piece if piece.shape[0] == HDIM else piece.at[pl.ds(i * HDIM, HDIM), :]
            copy = pltpu.make_async_copy(source, whole.at[pl.ds(row, HDIM), :], sems.at[len(copies)])
            copy.start()
            copies.append(copy)
    return copies


def assemble_kernel(heads, *refs):
    pieces, whole, sems = refs[:-2], refs[-2], refs[-1]
    for copy in place_heads(heads, 16, pieces, whole, sems):
        copy.wait()


def assemble(heads, pieces):
    return pl.pallas_call(
        assemble_kernel,
        out_shape=jax.ShapeDtypeStruct((8 * HDIM, pieces[0].shape[1]), bf16),
        in_specs=[IN_SMEM] + [pl.BlockSpec(memory_space=pl.ANY)] * len(pieces),
        out_specs=IN_VMEM,
        scratch_shapes=[pltpu.SemaphoreType.DMA((8,))],
        compiler_params=pltpu.CompilerParams(vmem_limit_bytes=5 << 20),
        name="assemble",
    )(heads, *pieces)


def join_kernel(*refs):
    halves, whole, sems = refs[:-2], refs[-2], refs[-1]
    rows = halves[0].shape[0]
    copies = [
        pltpu.make_async_copy(half, whole.at[pl.ds(i * rows, rows), :], sems.at[i])
        for i, half in enumerate(halves)
    ]
    for copy in copies:
        copy.start()
    for copy in copies:
        copy.wait()


def join(halves):
    rows, width = halves[0].shape
    return pl.pallas_call(
        join_kernel,
        out_shape=jax.ShapeDtypeStruct((len(halves) * rows, width), bf16),
        in_specs=[pl.BlockSpec(memory_space=pl.ANY)] * len(halves),
        out_specs=IN_VMEM,
        scratch_shapes=[pltpu.SemaphoreType.DMA((len(halves),))],
        compiler_params=pltpu.CompilerParams(vmem_limit_bytes=5 << 20),
        name="join",
    )(*halves)


def project_kernel(count, heads, *refs):
    pieces = refs[:10]
    (weight, gain, shift, proj, proj_bias, out, attended, normed, sems) = refs[10:]
    copies = place_heads(heads, 0, pieces, attended, sems)
    width = weight.shape[1]
    step = 512
    bias_column = jnp.broadcast_to(proj_bias[...], (8, proj.shape[0])).T[:, 0:1]
    for copy in copies:
        copy.wait()
    for b in range(count // step):
        turned = attended[:, b * step : (b + 1) * step].T
        rows = jnp.dot(turned, weight[...], preferred_element_type=f32).astype(bf16).astype(f32)
        rows = rows - jnp.sum(rows, axis=1, keepdims=True) * (1.0 / width)
        spread = jnp.sum(rows * rows, axis=1, keepdims=True) * (1.0 / width)
        rows = rows * lax.rsqrt(spread + EPSILON) * gain[...] + shift[...]
        for k in range(width // 128):
            normed[b, k] = rows[:, k * 128 : (k + 1) * 128]
        linear = jnp.zeros((proj.shape[0], step // 4), f32)
        for r in range(4):
            every_fourth = pl.ds(r, step // 4, stride=4)
            tokens = jnp.concatenate(
                [normed[b, k, every_fourth, :].astype(bf16) for k in range(width // 128)], axis=1
            )
            linear = linear + lax.dot_general(
                proj[:, r * width : (r + 1) * width],
                tokens,
                (((1,), (1,)), ((), ())),
                preferred_element_type=f32,
            )
        linear = linear + bias_column
        active = 0.5 * linear * (1.0 + lax.erf(linear * (0.5**0.5)))
        out[:, b * (step // 4) : (b + 1) * (step // 4)] = active.astype(bf16)


def project(heads, pieces, weight, gain, shift, proj, proj_bias):
    count = pieces[0].shape[1]
    depth, width = weight.shape
    return pl.pallas_call(
        functools.partial(project_kernel, count),
        out_shape=jax.ShapeDtypeStruct((proj.shape[0], count // 4), bf16),
        in_specs=[IN_SMEM] + [pl.BlockSpec(memory_space=pl.ANY)] * 10 + [IN_VMEM] * 5,
        out_specs=IN_VMEM,
        scratch_shapes=[
            pltpu.VMEM((depth, count), bf16),
            pltpu.VMEM((count // 512, width // 128, 512, 128), f32),
            pltpu.SemaphoreType.DMA((16,)),
        ],
        compiler_params=pltpu.CompilerParams(vmem_limit_bytes=30 << 20),
        name="project",
    )(heads, *pieces, weight, gain, shift, proj, proj_bias)


def head_order():
    table = []
    for x in range(4):
        for c in range(2):
            for t in range(2):

                def slot(a, d, b):
                    return (d != c) * 8 + a % 4 * 2 + b

                row = [slot(x, c, t), slot(x, 1 - c, t)]
                for d in (c, 1 - c):
                    side = x + (3, 1)[d]
                    cross = (x + 2, t) if d == 0 else (x, 1 - t)
                    row += [slot(side, d, t), slot(side, 1 - d, t)]
                    row += [slot(cross[0], d, cross[1]), slot(cross[0], 1 - d, cross[1])]
                    row += [slot(side, d, 1 - t), slot(side, 1 - d, 1 - t)]
                    row += [slot(x + 2, d, 1 - t)]
                for a in (x, x + 3, x + 1, x + 2):
                    row += [slot(a, c, t), slot(a, c, 1 - t)]
                table.append(row)
    return table


def on_device(
    queries, keys, values, segment_ids, out_weight, norm_gain, norm_bias, proj_weight, proj_bias
):
    blocks = lax.axis_size("blk")
    query_block, key_block = pack(queries.T, keys.T, values.T, segment_ids[None, :])

    sections = lax.axis_size("section")

    def swap(block, mask):
        if mask == 0:
            return block
        perm = []
        for i in range(blocks):
            for section in range(sections):
                turn = section % 2
                y, z = i // 8 ^ mask >> 3, ((i % 8 - turn) % 8 ^ mask & 7) + turn
                perm.append((i * sections + section, (y * 8 + z % 8) * sections + section))
        return lax.ppermute(block, ("blk", "section"), perm)

    def send(block, to):
        perm = []
        for x in range(4):
            for c in range(2):
                for t in range(2):
                    a, b, d = to(x, c, t)
                    perm.append(((x * 2 + c) * 2 + t, (a % 4 * 2 + b) * 2 + d))
        return lax.ppermute(block, GROUP, perm)

    me = lax.axis_index("section") * 2 + lax.axis_index("tp")
    heads = jnp.asarray(head_order(), jnp.int32)[me]

    def across(x, c, t):
        return x, 1 - c, t

    key_blocks = [swap(key_block, mask) for mask in KEY_PARTNERS]
    queries_at = [query_block, swap(query_block, QUERY_PARTNERS[1])]
    late_query, late_weight, _ = lax.optimization_barrier(
        (query_block, out_weight, (key_blocks, queries_at[1]))
    )
    queries_at += [swap(late_query, mask) for mask in QUERY_PARTNERS[2:]]
    far = send(late_weight, lambda x, c, t: (x, c, 1 - t))
    returned, held = attend(queries_at[:2], key_blocks)
    both = jnp.concatenate([late_weight, far], axis=0)
    returned[1] = swap(returned[1], QUERY_PARTNERS[1])
    both, late_queries, held = lax.optimization_barrier((both, queries_at[2:], held))
    weights = [both] + [send(both, lambda x, c, t, d=d: (x + d, c, t)) for d in (1, 3, 2)]
    late, _ = attend(late_queries, None, held)
    returned += [swap(part, mask) for part, mask in zip(late, QUERY_PARTNERS[2:])]
    weights, late = lax.optimization_barrier((weights, late))
    half = assemble(heads, weights)
    returned, half = lax.optimization_barrier((returned, half))
    other_half = send(half, across)
    attended = combine(returned)

    def along(x, c, t):
        return x + (1, -1)[c], c, t

    def along_far(x, c, t):
        return x + (1, -1)[c], c, 1 - t

    def opposite(x, c, t):
        return (x + 2, c, t) if c == 0 else (x, c, 1 - t)

    def opposite_far(x, c, t):
        return x + 2, c, 1 - t

    sibling = send(attended, across)
    pair = jnp.concatenate([attended, sibling], axis=0)
    received = [send(pair, along), send(pair, opposite), send(pair, along_far)]
    received.append(send(attended, opposite_far))
    weight, received[-1] = lax.optimization_barrier((join([half, other_half]), received[-1]))
    forwarded = [send(block, across) for block in received]
    pieces = [attended, sibling] + received + forwarded
    projected = project(
        heads,
        pieces,
        weight,
        norm_gain[None, :],
        norm_bias[None, :],
        proj_weight.T,
        proj_bias[None, :],
    )
    return projected.T


def solution(mesh):
    placed = (
        P("blk", GROUP),
        P("blk", GROUP),
        P("blk", GROUP),
        P("blk"),
        P(GROUP, None),
        P(),
        P(),
        P(None, GROUP),
        P(GROUP),
    )
    return jax.shard_map(
        on_device,
        mesh=mesh,
        in_specs=placed,
        out_specs=P("blk", GROUP),
        check_vma=False,
    )
```

```python
import functools

import jax
import jax.numpy as jnp
from jax import lax
from jax.experimental import pallas as pl
from jax.experimental.pallas import tpu as pltpu
from jax.sharding import PartitionSpec as P

HDIM = 80
EPSILON = 1e-06
EXP2_SCALE = 1.4426950408889634 * HDIM ** (-0.5)
MASKED = -1e30
NO_MAX = -1e20
MOST_EXCESS = 60.0 / EXP2_SCALE
KEY_PARTNERS = (0, 1, 8, 9)
QUERY_PARTNERS = (0, 4, 10, 14)
f32, bf16 = jnp.float32, jnp.bfloat16
GROUP = ("section", "tp")
IN_VMEM = pl.BlockSpec(memory_space=pltpu.VMEM)


def pack_kernel(queries, keys, values, ids, query_block, key_block, held_ids, sems):
    count = queries.shape[1]
    moves = [
        (ids, held_ids),
        (queries, query_block.at[0:80, :]),
        (keys, key_block.at[0:80, :]),
        (values, key_block.at[80:160, :]),
    ]
    copies = [pltpu.make_async_copy(*move, sems.at[i]) for i, move in enumerate(moves)]
    for copy in copies:
        copy.start()
    copies[0].wait()
    id_row = held_ids[...].astype(f32)
    zeros = jnp.zeros((6, count), f32)
    query_block[80:88, :] = jnp.concatenate([id_row, id_row, zeros], axis=0).astype(bf16)
    key_block[160:168, :] = jnp.concatenate([jnp.ones_like(id_row), id_row, zeros], axis=0).astype(bf16)
    for copy in copies[1:]:
        copy.wait()


def pack(queries, keys, values, ids):
    count = queries.shape[1]
    return pl.pallas_call(
        pack_kernel,
        out_shape=[
            jax.ShapeDtypeStruct((88, count), bf16),
            jax.ShapeDtypeStruct((168, count), bf16),
        ],
        in_specs=[pl.BlockSpec(memory_space=pltpu.HBM)] * 4,
        out_specs=[IN_VMEM] * 2,
        scratch_shapes=[pltpu.VMEM((1, count), jnp.int32), pltpu.SemaphoreType.DMA((4,))],
        compiler_params=pltpu.CompilerParams(vmem_limit_bytes=4 << 20),
        name="pack",
    )(*(pltpu.with_memory_space_constraint(x, pltpu.HBM) for x in (queries, keys, values, ids)))


def attend_block(query, held_k, held_v, limits, which, row_max, total, excess):
    count = query.shape[1]
    tiles, sub = 2, 256
    q_low, q_high = limits[which, 0], limits[which, 3]

    def tile(kb, start, tile_keys, masked, raising):
        rows = pl.ds(start, tile_keys)
        key_tile = held_k[kb, rows, :]
        value_tile = held_v[kb, :, rows]
        if masked:
            key_ids = jnp.broadcast_to(value_tile[80:88, :].T.astype(f32)[:, 1:2], (tile_keys, sub))

        def score(j):
            columns = slice(j * sub, (j + 1) * sub)
            found = jnp.dot(key_tile, query[0:80, columns], preferred_element_type=f32)
            if masked:
                query_ids = query[80:88, columns].astype(f32)[0:1, :]
                found = jnp.where(key_ids == query_ids, found, MASKED)
            return found

        scores = score(0)
        for j in range(count // sub):
            following = score(j + 1) if (j + 1) * sub < count else None
            columns = slice(j * sub, (j + 1) * sub)
            old = row_max[:, columns]
            if raising:
                new = jnp.maximum(old, jnp.max(scores, axis=0, keepdims=True))
                weights = jnp.exp2((scores - new) * EXP2_SCALE).astype(bf16)
                rescale = jnp.exp2((old - new) * EXP2_SCALE)
                total[:, columns] = total[:, columns] * rescale + jnp.dot(
                    value_tile, weights, preferred_element_type=f32
                )
                row_max[:, columns] = new
            else:
                weights = jnp.exp2((scores - old) * EXP2_SCALE).astype(bf16)
                total[:, columns] = total[:, columns] + jnp.dot(
                    value_tile, weights, preferred_element_type=f32
                )
                above = jnp.max(scores, axis=0, keepdims=True) - old
                excess[:, columns] = jnp.maximum(excess[:, columns], above)
            scores = following

    def every_key_block(keep_shift):
        row_max[...] = jnp.full_like(row_max, NO_MAX)
        total[...] = jnp.zeros_like(total)
        excess[...] = jnp.zeros_like(excess)

        def key_block_step(kb, started):
            low, high = limits[4 + kb, 0], limits[4 + kb, 3]
            live = jnp.logical_and(low <= q_high, high >= q_low)
            pure = q_low == q_high
            still = jnp.logical_and(
                jnp.logical_and(pure, jnp.logical_and(low == high, low == q_low)), keep_shift
            )

            @pl.when(jnp.logical_and(still, started == 0))
            def _():
                for j in range(count // sub):
                    columns = slice(j * sub, (j + 1) * sub)
                    found = jnp.dot(held_k[kb, 0:128, :], query[0:80, columns], preferred_element_type=f32)
                    row_max[:, columns] = jnp.max(found, axis=0, keepdims=True)

            @pl.when(still)
            def _():
                tile(kb, 0, count, False, False)

            @pl.when(jnp.logical_and(live, jnp.logical_not(still)))
            def _():
                def half(t, unused):
                    low, high = limits[4 + kb, 2 * t], limits[4 + kb, 2 * t + 1]

                    @pl.when(jnp.logical_and(low <= q_high, high >= q_low))
                    def _():
                        tile(kb, pl.multiple_of(t * (count // tiles), 128), count // tiles, True, True)

                    return 0

                lax.fori_loop(0, tiles, half, 0)

            return jnp.maximum(started, live.astype(jnp.int32))

        lax.fori_loop(0, 4, key_block_step, 0)

    def attempt(tried, unused):
        @pl.when(jnp.logical_or(tried == 0, jnp.max(excess[...]) > MOST_EXCESS))
        def _():
            every_key_block(tried == 0)

        return 0

    lax.fori_loop(0, 2, attempt, 0)


def store_partial(out, row_max, total):
    def split(value, parts):
        pieces = []
        for _ in range(parts):
            piece = value.astype(bf16).astype(f32)
            pieces.append(piece)
            value = value - piece
        return pieces

    rows = split(total[80:81, :], 2) + split(row_max[...], 3)
    rows.append(jnp.zeros((3, out.shape[1]), f32))
    out[0:80, :] = total[0:80, :].astype(bf16)
    out[80:88, :] = jnp.concatenate(rows, axis=0).astype(bf16)


def find_limits(ids, limits, limits_s, sem):
    count = ids.shape[1]
    lane = lax.broadcasted_iota(jnp.int32, (8, 128), 1)
    table = jnp.zeros((8, 128), f32)
    for t in range(2):
        part = ids[:, t * (count // 2) : (t + 1) * (count // 2)]
        table = jnp.where(lane == 2 * t, jnp.min(part, axis=1, keepdims=True), table)
        table = jnp.where(lane == 2 * t + 1, jnp.max(part, axis=1, keepdims=True), table)
    limits[...] = table.astype(jnp.int32)
    copy = pltpu.make_async_copy(limits, limits_s, sem)
    copy.start()
    copy.wait()


def attend_kernel(blocks, first, *refs):
    queries, refs = refs[:blocks], refs[blocks:]
    if first:
        key_values, refs = refs[:4], refs[4:]
    else:
        (held_k, held_v), refs = refs[:2], refs[2:]
    outs, refs = refs[:blocks], refs[blocks:]
    if first:
        (held_k, held_v), refs = refs[:2], refs[2:]
    query, ids, limits, limits_s, row_max, total, excess, sem = refs
    ids[...] = jnp.zeros_like(ids)
    for i in range(4):
        if first:
            held_k[i] = key_values[i][0:80, :].T
            held_v[i] = key_values[i][80:168, :]
        ids[4 + i : 5 + i, :] = held_v[i, 80:88, :].astype(f32)[1:2, :]
    for i in range(blocks):
        query[i] = queries[i][...]
        ids[i : i + 1, :] = queries[i][80:88, :].astype(f32)[0:1, :]
    find_limits(ids, limits, limits_s, sem)

    def one(i, unused):
        attend_block(query.at[i], held_k, held_v, limits_s, i, row_max, total, excess)
        for o in range(blocks):

            @pl.when(i == o)
            def _():
                store_partial(outs[o], row_max, total)

        return 0

    lax.fori_loop(0, blocks, one, 0)


def attend(queries, key_values, held=None):
    count = queries[0].shape[1]
    first = held is None
    shapes = [jax.ShapeDtypeStruct((88, count), bf16)] * len(queries)
    if first:
        shapes.append(jax.ShapeDtypeStruct((4, count, 80), bf16))
        shapes.append(jax.ShapeDtypeStruct((4, 88, count), bf16))
    operands = list(queries) + list(key_values if first else held)
    out = pl.pallas_call(
        functools.partial(attend_kernel, len(queries), first),
        out_shape=shapes,
        in_specs=[IN_VMEM] * len(operands),
        out_specs=[IN_VMEM] * len(shapes),
        scratch_shapes=[
            pltpu.VMEM((len(queries), 88, count), bf16),
            pltpu.VMEM((8, count), f32),
            pltpu.VMEM((8, 128), jnp.int32),
            pltpu.SMEM((8, 128), jnp.int32),
            pltpu.VMEM((1, count), f32),
            pltpu.VMEM((88, count), f32),
            pltpu.VMEM((1, count), f32),
            pltpu.SemaphoreType.DMA,
        ],
        compiler_params=pltpu.CompilerParams(vmem_limit_bytes=16 << 20),
        name="attend_first" if first else "attend_next",
    )(*operands)
    return list(out[: len(queries)]), list(out[len(queries) :])


def this_core():
    return lax.rem(lax.axis_index("section"), 2)


def combine_kernel(*refs):
    parts, (mine, others, whole) = refs[:4], refs[4:]
    core = this_core()
    sums, maxima = [], []
    for part in parts:
        rows = part[80:88, :].astype(f32)
        sums.append(rows[0:1, :] + rows[1:2, :])
        maxima.append((rows[2:3, :] + rows[3:4, :]) + rows[4:5, :])
    top = functools.reduce(jnp.maximum, maxima)
    factors = [jnp.exp2((m - top) * EXP2_SCALE) for m in maxima]
    inverse = 1.0 / functools.reduce(jnp.add, [w * s for w, s in zip(factors, sums)])
    mixed = functools.reduce(
        jnp.add, [part[0:80, :].astype(f32) * w for part, w in zip(parts, factors)]
    )
    whole[...] = (mixed * inverse).astype(bf16)
    half = mine.shape[1]
    mine[...] = whole[:, pl.ds(pl.multiple_of(core * half, 128), half)]
    others[...] = whole[:, pl.ds(pl.multiple_of((1 - core) * half, 128), half)]


def combine(parts):
    count = parts[0].shape[1]
    return pl.pallas_call(
        combine_kernel,
        out_shape=[jax.ShapeDtypeStruct((80, count // 2), bf16)] * 2,
        in_specs=[IN_VMEM] * 4,
        out_specs=[IN_VMEM] * 2,
        scratch_shapes=[pltpu.VMEM((80, count), bf16)],
        compiler_params=pltpu.CompilerParams(vmem_limit_bytes=6 << 20),
        name="combine",
    )(*parts)


def copies_kernel(moves, *refs):
    sources, whole, sems = refs[:-2], refs[-2], refs[-1]
    copies = []
    for i, (source, start, target, rows) in enumerate(moves):
        copies.append(
            pltpu.make_async_copy(
                sources[source].at[start : start + rows, :],
                whole.at[target : target + rows, :],
                sems.at[i],
            )
        )
        copies[-1].start()
    for copy in copies:
        copy.wait()


def place_rows(sources, moves, name):
    rows = sum(move[3] for move in moves)
    return pl.pallas_call(
        functools.partial(copies_kernel, moves),
        out_shape=jax.ShapeDtypeStruct((rows, sources[0].shape[1]), bf16),
        in_specs=[pl.BlockSpec(memory_space=pl.ANY)] * len(sources),
        out_specs=IN_VMEM,
        scratch_shapes=[pltpu.SemaphoreType.DMA((len(moves),))],
        compiler_params=pltpu.CompilerParams(vmem_limit_bytes=5 << 20),
        name=name,
    )(*sources)


def project_kernel(*refs):
    pieces = refs[:8]
    (weight, gain, shift, *projs, out_mine, out_others, normed) = refs[8:]
    width = weight.shape[1]
    count = pieces[0].shape[1]
    attended = jnp.concatenate([piece[...] for piece in pieces], axis=0)
    rows = jnp.dot(attended.T, weight[...], preferred_element_type=f32).astype(bf16).astype(f32)
    rows = rows - jnp.sum(rows, axis=1, keepdims=True) * (1.0 / width)
    spread = jnp.sum(rows * rows, axis=1, keepdims=True) * (1.0 / width)
    rows = rows * lax.rsqrt(spread + EPSILON) * gain[...] + shift[...]
    for k in range(width // 128):
        normed[k] = rows[:, k * 128 : (k + 1) * 128]
    tokens = []
    for r in range(4):
        every_fourth = pl.ds(r, count // 4, stride=4)
        tokens.append(
            jnp.concatenate(
                [normed[k, every_fourth, :].astype(bf16) for k in range(width // 128)], axis=1
            )
        )
    for out, proj, bias in ((out_others, projs[2], projs[3]), (out_mine, projs[0], projs[1])):
        linear = jnp.broadcast_to(bias[...], (8, proj.shape[0])).T[:, 0:1]
        for r in range(4):
            linear = linear + lax.dot_general(
                proj[:, r * width : (r + 1) * width],
                tokens[r],
                (((1,), (1,)), ((), ())),
                preferred_element_type=f32,
            )
        out[...] = (0.5 * linear * (1.0 + lax.erf(linear * (0.5**0.5)))).astype(bf16)


def project(pieces, weight, gain, shift, mine, others):
    count, width = pieces[0].shape[1], weight.shape[1]
    return pl.pallas_call(
        project_kernel,
        out_shape=[jax.ShapeDtypeStruct((mine[0].shape[0], count // 4), bf16)] * 2,
        in_specs=[IN_VMEM] * 15,
        out_specs=[IN_VMEM] * 2,
        scratch_shapes=[pltpu.VMEM((width // 128, count, 128), f32)],
        compiler_params=pltpu.CompilerParams(vmem_limit_bytes=24 << 20),
        name="project",
    )(*pieces, weight, gain, shift, *mine, *others)


def finish_kernel(mine, rest, out):
    core, count = this_core(), mine.shape[1]
    out[:, pl.ds(pl.multiple_of(core * count, 128), count)] = mine[...]
    out[:, pl.ds(pl.multiple_of((1 - core) * count, 128), count)] = rest[...]


def finish(mine, rest):
    rows, count = mine.shape
    return pl.pallas_call(
        finish_kernel,
        out_shape=jax.ShapeDtypeStruct((rows, 2 * count), bf16),
        in_specs=[IN_VMEM] * 2,
        out_specs=IN_VMEM,
        compiler_params=pltpu.CompilerParams(vmem_limit_bytes=4 << 20),
        name="finish",
    )(mine, rest)


def on_device(
    queries, keys, values, segment_ids, out_weight, norm_gain, norm_bias, proj_weight, proj_bias
):
    blocks = lax.axis_size("blk")
    query_block, key_block = pack(queries.T, keys.T, values.T, segment_ids[None, :])

    sections = lax.axis_size("section")

    def swap(block, mask):
        if mask == 0:
            return block
        perm = []
        for i in range(blocks):
            for section in range(sections):
                turn = section % 2
                y, z = i // 8 ^ mask >> 3, ((i % 8 - turn) % 8 ^ mask & 7) + turn
                perm.append((i * sections + section, (y * 8 + z % 8) * sections + section))
        return lax.ppermute(block, ("blk", "section"), perm)

    def send(block, to):
        perm = []
        for x in range(4):
            for c in range(2):
                for t in range(2):
                    a, b, d = to(x, c, t)
                    perm.append(((x * 2 + c) * 2 + t, (a % 4 * 2 + b) * 2 + d))
        return lax.ppermute(block, GROUP, perm)

    def across(x, c, t):
        return x, 1 - c, t

    key_blocks = [swap(key_block, mask) for mask in KEY_PARTNERS]
    queries_at = [query_block, swap(query_block, QUERY_PARTNERS[1])]
    late_query, late_weight, late_proj, late_bias, _ = lax.optimization_barrier(
        (query_block, out_weight, proj_weight, proj_bias, (key_blocks, queries_at[1]))
    )
    queries_at += [swap(late_query, mask) for mask in QUERY_PARTNERS[2:]]
    far = send(late_weight, lambda x, c, t: (x, c, 1 - t))
    mine = (late_proj.T, late_bias[None, :])
    others = tuple(send(block, across) for block in mine)
    returned, held = attend(queries_at[:2], key_blocks)
    both = place_rows([late_weight, far], [(i, 0, i * HDIM, HDIM) for i in range(2)], "both")
    returned[1] = swap(returned[1], QUERY_PARTNERS[1])
    both, others, late_queries, held = lax.optimization_barrier((both, others, queries_at[2:], held))
    steps = (1, 3, 2)
    weights = [both] + [send(both, lambda x, c, t, d=d: (x + d, c, t)) for d in steps]
    late, _ = attend(late_queries, None, held)
    returned += [swap(part, mask) for part, mask in zip(late, QUERY_PARTNERS[2:])]
    weights, late = lax.optimization_barrier((weights, late))
    half = place_rows(weights, [(i, 0, i * 160, 160) for i in range(4)], "assemble")
    returned, half = lax.optimization_barrier((returned, half))
    other_half = send(half, across)
    kept, given = combine(returned)

    pair = place_rows([kept, send(given, across)], [(i, 0, i * HDIM, HDIM) for i in range(2)], "pair")
    pieces = {(0, 0): pair}
    for d, e in ((2, 1), (1, 1), (3, 1), (2, 0), (0, 1), (1, 0), (3, 0)):
        pieces[d, e] = send(pair, lambda x, c, t: (x + d, c, (t + e) % 2))
    order = [(d, e) for d in (0,) + steps for e in (0, 1)]
    moves = [(h, i * HDIM, (2 * i + h) * HDIM, HDIM) for i in range(8) for h in range(2)]
    weight = place_rows([half, other_half], moves, "join")
    weight, pieces[3, 0] = lax.optimization_barrier((weight, pieces[3, 0]))
    out_mine, out_others = project(
        [pieces[place] for place in order],
        weight,
        norm_gain[None, :],
        norm_bias[None, :],
        mine,
        others,
    )
    return finish(out_mine, send(out_others, across)).T


def solution(mesh):
    placed = (
        P("blk", GROUP),
        P("blk", GROUP),
        P("blk", GROUP),
        P("blk"),
        P(GROUP, None),
        P(),
        P(),
        P(None, GROUP),
        P(GROUP),
    )
    return jax.shard_map(
        on_device,
        mesh=mesh,
        in_specs=placed,
        out_specs=P("blk", GROUP),
        check_vma=False,
    )
```

```python
import functools

import jax
import jax.numpy as jnp
from jax import lax
from jax.experimental import pallas as pl
from jax.experimental.pallas import tpu as pltpu
from jax.sharding import PartitionSpec as P

HDIM = 80
EPSILON = 1e-06
EXP2_SCALE = 1.4426950408889634 * HDIM ** (-0.5)
MASKED = -1e30
NO_MAX = -1e20
MOST_EXCESS = 60.0 / EXP2_SCALE
KEY_PARTNERS = (0, 1, 8, 9)
QUERY_PARTNERS = (0, 4, 10, 14)
f32, bf16 = jnp.float32, jnp.bfloat16
GROUP = ("section", "tp")
IN_VMEM = pl.BlockSpec(memory_space=pltpu.VMEM)


def pack_kernel(queries, keys, values, ids, query_block, key_block, held_ids, sems):
    count = queries.shape[1]
    moves = [
        (ids, held_ids),
        (queries, query_block.at[0:80, :]),
        (keys, key_block.at[0:80, :]),
        (values, key_block.at[80:160, :]),
    ]
    copies = [pltpu.make_async_copy(*move, sems.at[i]) for i, move in enumerate(moves)]
    for copy in copies:
        copy.start()
    copies[0].wait()
    id_row = held_ids[...].astype(f32)
    zeros = jnp.zeros((6, count), f32)
    query_block[80:88, :] = jnp.concatenate([id_row, id_row, zeros], axis=0).astype(bf16)
    key_block[160:168, :] = jnp.concatenate([jnp.ones_like(id_row), id_row, zeros], axis=0).astype(bf16)
    for copy in copies[1:]:
        copy.wait()


def pack(queries, keys, values, ids):
    count = queries.shape[1]
    return pl.pallas_call(
        pack_kernel,
        out_shape=[
            jax.ShapeDtypeStruct((88, count), bf16),
            jax.ShapeDtypeStruct((168, count), bf16),
        ],
        in_specs=[pl.BlockSpec(memory_space=pltpu.HBM)] * 4,
        out_specs=[IN_VMEM] * 2,
        scratch_shapes=[pltpu.VMEM((1, count), jnp.int32), pltpu.SemaphoreType.DMA((4,))],
        compiler_params=pltpu.CompilerParams(vmem_limit_bytes=4 << 20),
        name="pack",
    )(*(pltpu.with_memory_space_constraint(x, pltpu.HBM) for x in (queries, keys, values, ids)))


def attend_block(query, held_k, held_v, limits, which, row_max, total, excess):
    count = query.shape[1]
    tiles, sub = 2, 256
    q_low, q_high = limits[which, 0], limits[which, 3]

    def tile(kb, start, tile_keys, masked, raising):
        rows = pl.ds(start, tile_keys)
        key_tile = held_k[kb, rows, :]
        value_tile = held_v[kb, :, rows]
        if masked:
            key_ids = jnp.broadcast_to(value_tile[80:88, :].T.astype(f32)[:, 1:2], (tile_keys, sub))

        def score(j):
            columns = slice(j * sub, (j + 1) * sub)
            found = jnp.dot(key_tile, query[0:80, columns], preferred_element_type=f32)
            if masked:
                query_ids = query[80:88, columns].astype(f32)[0:1, :]
                found = jnp.where(key_ids == query_ids, found, MASKED)
            return found

        scores = score(0)
        for j in range(count // sub):
            following = score(j + 1) if (j + 1) * sub < count else None
            columns = slice(j * sub, (j + 1) * sub)
            old = row_max[:, columns]
            if raising:
                new = jnp.maximum(old, jnp.max(scores, axis=0, keepdims=True))
                weights = jnp.exp2((scores - new) * EXP2_SCALE).astype(bf16)
                rescale = jnp.exp2((old - new) * EXP2_SCALE)
                total[:, columns] = total[:, columns] * rescale + jnp.dot(
                    value_tile, weights, preferred_element_type=f32
                )
                row_max[:, columns] = new
            else:
                weights = jnp.exp2((scores - old) * EXP2_SCALE).astype(bf16)
                total[:, columns] = total[:, columns] + jnp.dot(
                    value_tile, weights, preferred_element_type=f32
                )
                above = jnp.max(scores, axis=0, keepdims=True) - old
                excess[:, columns] = jnp.maximum(excess[:, columns], above)
            scores = following

    def every_key_block(keep_shift):
        row_max[...] = jnp.full_like(row_max, NO_MAX)
        total[...] = jnp.zeros_like(total)
        excess[...] = jnp.zeros_like(excess)

        def key_block_step(kb, started):
            low, high = limits[4 + kb, 0], limits[4 + kb, 3]
            live = jnp.logical_and(low <= q_high, high >= q_low)
            pure = q_low == q_high
            still = jnp.logical_and(
                jnp.logical_and(pure, jnp.logical_and(low == high, low == q_low)), keep_shift
            )

            @pl.when(jnp.logical_and(still, started == 0))
            def _():
                for j in range(count // sub):
                    columns = slice(j * sub, (j + 1) * sub)
                    found = jnp.dot(held_k[kb, 0:128, :], query[0:80, columns], preferred_element_type=f32)
                    row_max[:, columns] = jnp.max(found, axis=0, keepdims=True)

            @pl.when(still)
            def _():
                tile(kb, 0, count, False, False)

            @pl.when(jnp.logical_and(live, jnp.logical_not(still)))
            def _():
                def half(t, unused):
                    low, high = limits[4 + kb, 2 * t], limits[4 + kb, 2 * t + 1]

                    @pl.when(jnp.logical_and(low <= q_high, high >= q_low))
                    def _():
                        tile(kb, pl.multiple_of(t * (count // tiles), 128), count // tiles, True, True)

                    return 0

                lax.fori_loop(0, tiles, half, 0)

            return jnp.maximum(started, live.astype(jnp.int32))

        lax.fori_loop(0, 4, key_block_step, 0)

    def attempt(tried, unused):
        @pl.when(jnp.logical_or(tried == 0, jnp.max(excess[...]) > MOST_EXCESS))
        def _():
            every_key_block(tried == 0)

        return 0

    lax.fori_loop(0, 2, attempt, 0)


def store_partial(out, row_max, total):
    def split(value, parts):
        pieces = []
        for _ in range(parts):
            piece = value.astype(bf16).astype(f32)
            pieces.append(piece)
            value = value - piece
        return pieces

    rows = split(total[80:81, :], 2) + split(row_max[...], 3)
    rows.append(jnp.zeros((3, out.shape[1]), f32))
    out[0:80, :] = total[0:80, :].astype(bf16)
    out[80:88, :] = jnp.concatenate(rows, axis=0).astype(bf16)


def find_limits(ids, limits, limits_s, sem):
    count = ids.shape[1]
    lane = lax.broadcasted_iota(jnp.int32, (8, 128), 1)
    table = jnp.zeros((8, 128), f32)
    for t in range(2):
        part = ids[:, t * (count // 2) : (t + 1) * (count // 2)]
        table = jnp.where(lane == 2 * t, jnp.min(part, axis=1, keepdims=True), table)
        table = jnp.where(lane == 2 * t + 1, jnp.max(part, axis=1, keepdims=True), table)
    limits[...] = table.astype(jnp.int32)
    copy = pltpu.make_async_copy(limits, limits_s, sem)
    copy.start()
    copy.wait()


def attend_kernel(blocks, first, *refs):
    queries, refs = refs[:blocks], refs[blocks:]
    if first:
        key_values, refs = refs[:4], refs[4:]
    else:
        (held_k, held_v), refs = refs[:2], refs[2:]
    outs, refs = refs[:blocks], refs[blocks:]
    if first:
        (held_k, held_v), refs = refs[:2], refs[2:]
    query, ids, limits, limits_s, row_max, total, excess, sem = refs
    ids[...] = jnp.zeros_like(ids)
    for i in range(4):
        if first:
            held_k[i] = key_values[i][0:80, :].T
            held_v[i] = key_values[i][80:168, :]
        ids[4 + i : 5 + i, :] = held_v[i, 80:88, :].astype(f32)[1:2, :]
    for i in range(blocks):
        query[i] = queries[i][...]
        ids[i : i + 1, :] = queries[i][80:88, :].astype(f32)[0:1, :]
    find_limits(ids, limits, limits_s, sem)

    def one(i, unused):
        attend_block(query.at[i], held_k, held_v, limits_s, i, row_max, total, excess)
        for o in range(blocks):

            @pl.when(i == o)
            def _():
                store_partial(outs[o], row_max, total)

        return 0

    lax.fori_loop(0, blocks, one, 0)


def attend(queries, key_values, held=None):
    count = queries[0].shape[1]
    first = held is None
    shapes = [jax.ShapeDtypeStruct((88, count), bf16)] * len(queries)
    if first:
        shapes.append(jax.ShapeDtypeStruct((4, count, 80), bf16))
        shapes.append(jax.ShapeDtypeStruct((4, 88, count), bf16))
    operands = list(queries) + list(key_values if first else held)
    out = pl.pallas_call(
        functools.partial(attend_kernel, len(queries), first),
        out_shape=shapes,
        in_specs=[IN_VMEM] * len(operands),
        out_specs=[IN_VMEM] * len(shapes),
        scratch_shapes=[
            pltpu.VMEM((len(queries), 88, count), bf16),
            pltpu.VMEM((8, count), f32),
            pltpu.VMEM((8, 128), jnp.int32),
            pltpu.SMEM((8, 128), jnp.int32),
            pltpu.VMEM((1, count), f32),
            pltpu.VMEM((88, count), f32),
            pltpu.VMEM((1, count), f32),
            pltpu.SemaphoreType.DMA,
        ],
        compiler_params=pltpu.CompilerParams(vmem_limit_bytes=16 << 20),
        name="attend_first" if first else "attend_next",
    )(*operands)
    return list(out[: len(queries)]), list(out[len(queries) :])


def this_core():
    return lax.rem(lax.axis_index("section"), 2)


def combine_kernel(*refs):
    parts, (mine, others, whole) = refs[:4], refs[4:]
    core = this_core()
    sums, maxima = [], []
    for part in parts:
        rows = part[80:88, :].astype(f32)
        sums.append(rows[0:1, :] + rows[1:2, :])
        maxima.append((rows[2:3, :] + rows[3:4, :]) + rows[4:5, :])
    top = functools.reduce(jnp.maximum, maxima)
    factors = [jnp.exp2((m - top) * EXP2_SCALE) for m in maxima]
    inverse = 1.0 / functools.reduce(jnp.add, [w * s for w, s in zip(factors, sums)])
    mixed = functools.reduce(
        jnp.add, [part[0:80, :].astype(f32) * w for part, w in zip(parts, factors)]
    )
    whole[...] = (mixed * inverse).astype(bf16)
    half = mine.shape[1]
    mine[...] = whole[:, pl.ds(pl.multiple_of(core * half, 128), half)]
    others[...] = whole[:, pl.ds(pl.multiple_of((1 - core) * half, 128), half)]


def combine(parts):
    count = parts[0].shape[1]
    return pl.pallas_call(
        combine_kernel,
        out_shape=[jax.ShapeDtypeStruct((80, count // 2), bf16)] * 2,
        in_specs=[IN_VMEM] * 4,
        out_specs=[IN_VMEM] * 2,
        scratch_shapes=[pltpu.VMEM((80, count), bf16)],
        compiler_params=pltpu.CompilerParams(vmem_limit_bytes=6 << 20),
        name="combine",
    )(*parts)


def copies_kernel(moves, *refs):
    sources, whole, sems = refs[:-2], refs[-2], refs[-1]
    copies = []
    for i, (source, start, target, rows) in enumerate(moves):
        copies.append(
            pltpu.make_async_copy(
                sources[source].at[start : start + rows, :],
                whole.at[target : target + rows, :],
                sems.at[i],
            )
        )
        copies[-1].start()
    for copy in copies:
        copy.wait()


def place_rows(sources, moves, name, spaces=None):
    rows = sum(move[3] for move in moves)
    return pl.pallas_call(
        functools.partial(copies_kernel, moves),
        out_shape=jax.ShapeDtypeStruct((rows, sources[0].shape[1]), bf16),
        in_specs=[pl.BlockSpec(memory_space=space) for space in spaces or [pl.ANY] * len(sources)],
        out_specs=IN_VMEM,
        scratch_shapes=[pltpu.SemaphoreType.DMA((len(moves),))],
        compiler_params=pltpu.CompilerParams(vmem_limit_bytes=5 << 20),
        name=name,
    )(*sources)


def project_kernel(*refs):
    pieces = refs[:8]
    (weight, gain, shift, *projs, out_mine, out_others, normed) = refs[8:]
    width = weight.shape[1]
    count = pieces[0].shape[1]
    attended = jnp.concatenate([piece[...] for piece in pieces], axis=0)
    rows = jnp.dot(attended.T, weight[...], preferred_element_type=f32).astype(bf16).astype(f32)
    rows = rows - jnp.sum(rows, axis=1, keepdims=True) * (1.0 / width)
    spread = jnp.sum(rows * rows, axis=1, keepdims=True) * (1.0 / width)
    rows = rows * lax.rsqrt(spread + EPSILON) * gain[...] + shift[...]
    for k in range(width // 128):
        normed[k] = rows[:, k * 128 : (k + 1) * 128]
    tokens = []
    for r in range(4):
        every_fourth = pl.ds(r, count // 4, stride=4)
        tokens.append(
            jnp.concatenate(
                [normed[k, every_fourth, :].astype(bf16) for k in range(width // 128)], axis=1
            )
        )
    for out, proj in ((out_others, projs[1]), (out_mine, projs[0])):
        linear = jnp.zeros(out.shape, f32)
        for r in range(4):
            linear = linear + lax.dot_general(
                proj[:, r * width : (r + 1) * width],
                tokens[r],
                (((1,), (1,)), ((), ())),
                preferred_element_type=f32,
            )
        out[...] = linear


def project(pieces, weight, gain, shift, mine, others):
    count, width = pieces[0].shape[1], weight.shape[1]
    return pl.pallas_call(
        project_kernel,
        out_shape=[jax.ShapeDtypeStruct((mine.shape[0], count // 4), f32)] * 2,
        in_specs=[IN_VMEM] * 13,
        out_specs=[IN_VMEM] * 2,
        scratch_shapes=[pltpu.VMEM((width // 128, count, 128), f32)],
        compiler_params=pltpu.CompilerParams(vmem_limit_bytes=24 << 20),
        name="project",
    )(*pieces, weight, gain, shift, mine, others)


def finish_kernel(mine, rest, bias, out):
    core, count = this_core(), mine.shape[1]
    bias_column = jnp.broadcast_to(bias[...], (8, mine.shape[0])).T[:, 0:1]
    for place, product in ((core, mine), (1 - core, rest)):
        linear = product[...] + bias_column
        active = 0.5 * linear * (1.0 + lax.erf(linear * (0.5**0.5)))
        out[:, pl.ds(pl.multiple_of(place * count, 128), count)] = active.astype(bf16)


def finish(mine, rest, bias):
    rows, count = mine.shape
    return pl.pallas_call(
        finish_kernel,
        out_shape=jax.ShapeDtypeStruct((rows, 2 * count), bf16),
        in_specs=[IN_VMEM] * 3,
        out_specs=IN_VMEM,
        compiler_params=pltpu.CompilerParams(vmem_limit_bytes=4 << 20),
        name="finish",
    )(mine, rest, bias)


def on_device(
    queries, keys, values, segment_ids, out_weight, norm_gain, norm_bias, proj_weight, proj_bias
):
    blocks = lax.axis_size("blk")
    query_block, key_block = pack(queries.T, keys.T, values.T, segment_ids[None, :])

    sections = lax.axis_size("section")

    def swap(block, mask):
        if mask == 0:
            return block
        perm = []
        for i in range(blocks):
            for section in range(sections):
                turn = section % 2
                y, z = i // 8 ^ mask >> 3, ((i % 8 - turn) % 8 ^ mask & 7) + turn
                perm.append((i * sections + section, (y * 8 + z % 8) * sections + section))
        return lax.ppermute(block, ("blk", "section"), perm)

    def send(block, to):
        perm = []
        for x in range(4):
            for c in range(2):
                for t in range(2):
                    a, b, d = to(x, c, t)
                    perm.append(((x * 2 + c) * 2 + t, (a % 4 * 2 + b) * 2 + d))
        return lax.ppermute(block, GROUP, perm)

    def across(x, c, t):
        return x, 1 - c, t

    others = send(proj_weight.T, across)
    far = send(out_weight, lambda x, c, t: (x, c, 1 - t))
    key_blocks = [swap(key_block, mask) for mask in KEY_PARTNERS]
    far_query, others = lax.optimization_barrier((query_block, others))
    queries_at = [query_block, swap(far_query, QUERY_PARTNERS[1])]
    both = place_rows(
        [pltpu.with_memory_space_constraint(out_weight, pltpu.HBM), far],
        [(i, 0, i * HDIM, HDIM) for i in range(2)],
        "both",
        (pltpu.HBM, pl.ANY),
    )
    late_query, both, key_blocks, queries_at[1] = lax.optimization_barrier(
        (query_block, both, key_blocks, queries_at[1])
    )
    queries_at += [swap(late_query, mask) for mask in QUERY_PARTNERS[2:]]
    returned, held = attend(queries_at[:2], key_blocks)
    returned[1] = swap(returned[1], QUERY_PARTNERS[1])
    both, others, late_queries, held = lax.optimization_barrier((both, others, queries_at[2:], held))
    steps = (1, 3, 2)
    weights = [both] + [send(both, lambda x, c, t, d=d: (x + d, c, t)) for d in steps]
    late, _ = attend(late_queries, None, held)
    returned += [swap(part, mask) for part, mask in zip(late, QUERY_PARTNERS[2:])]
    weights, late = lax.optimization_barrier((weights, late))
    half = place_rows(weights, [(i, 0, i * 160, 160) for i in range(4)], "assemble")
    returned, half = lax.optimization_barrier((returned, half))
    other_half = send(half, across)
    kept, given = combine(returned)

    pair = place_rows([kept, send(given, across)], [(i, 0, i * HDIM, HDIM) for i in range(2)], "pair")
    pieces = {(0, 0): pair, (0, 1): send(pair, lambda x, c, t: (x, c, 1 - t))}
    for e in (0, 1):
        for d in (2, 1, 3):
            pieces[d, e] = send(pieces[0, e], lambda x, c, t: (x + d, c, t))
    order = [(d, e) for d in (0,) + steps for e in (0, 1)]
    moves = [(h, i * HDIM, (2 * i + h) * HDIM, HDIM) for i in range(8) for h in range(2)]
    weight = place_rows([half, other_half], moves, "join")
    out_mine, out_others = project(
        [pieces[place] for place in order],
        weight,
        norm_gain[None, :],
        norm_bias[None, :],
        proj_weight.T,
        others,
    )
    return finish(out_mine, send(out_others, across), proj_bias[None, :]).T


def solution(mesh):
    placed = (
        P("blk", GROUP),
        P("blk", GROUP),
        P("blk", GROUP),
        P("blk"),
        P(GROUP, None),
        P(),
        P(),
        P(None, GROUP),
        P(GROUP),
    )
    return jax.shard_map(
        on_device,
        mesh=mesh,
        in_specs=placed,
        out_specs=P("blk", GROUP),
        check_vma=False,
    )
```

```python
import functools

import jax
import jax.numpy as jnp
from jax import lax
from jax.experimental import pallas as pl
from jax.experimental.pallas import tpu as pltpu
from jax.sharding import PartitionSpec as P

HDIM = 80
EPSILON = 1e-06
EXP2_SCALE = 1.4426950408889634 * HDIM ** (-0.5)
MASKED = -1e30
NO_MAX = -1e20
MOST_EXCESS = 60.0 / EXP2_SCALE
KEY_PARTNERS = (0, 1, 8, 9)
QUERY_PARTNERS = (0, 4, 10, 14)
f32, bf16 = jnp.float32, jnp.bfloat16
GROUP = ("section", "tp")
IN_VMEM = pl.BlockSpec(memory_space=pltpu.VMEM)


def pack_kernel(queries, keys, values, ids, query_block, key_block, held_ids, sems):
    count = queries.shape[1]
    moves = [
        (ids, held_ids),
        (queries, query_block.at[0:80, :]),
        (keys, key_block.at[0:80, :]),
        (values, key_block.at[80:160, :]),
    ]
    copies = [pltpu.make_async_copy(*move, sems.at[i]) for i, move in enumerate(moves)]
    for copy in copies:
        copy.start()
    copies[0].wait()
    id_row = held_ids[...].astype(f32)
    zeros = jnp.zeros((6, count), f32)
    query_block[80:88, :] = jnp.concatenate([id_row, id_row, zeros], axis=0).astype(bf16)
    key_block[160:168, :] = jnp.concatenate([jnp.ones_like(id_row), id_row, zeros], axis=0).astype(bf16)
    for copy in copies[1:]:
        copy.wait()


def pack(queries, keys, values, ids):
    count = queries.shape[1]
    return pl.pallas_call(
        pack_kernel,
        out_shape=[
            jax.ShapeDtypeStruct((88, count), bf16),
            jax.ShapeDtypeStruct((168, count), bf16),
        ],
        in_specs=[pl.BlockSpec(memory_space=pltpu.HBM)] * 4,
        out_specs=[IN_VMEM] * 2,
        scratch_shapes=[pltpu.VMEM((1, count), jnp.int32), pltpu.SemaphoreType.DMA((4,))],
        compiler_params=pltpu.CompilerParams(vmem_limit_bytes=4 << 20),
        name="pack",
    )(*(pltpu.with_memory_space_constraint(x, pltpu.HBM) for x in (queries, keys, values, ids)))


def attend_block(query, held_k, held_v, limits, which, row_max, total, excess):
    count = query.shape[1]
    tiles, sub = 2, 256
    q_low, q_high = limits[which, 0], limits[which, 3]

    def tile(kb, start, tile_keys, masked, raising):
        rows = pl.ds(start, tile_keys)
        key_tile = held_k[kb, rows, :]
        value_tile = held_v[kb, :, rows]
        if masked:
            key_ids = jnp.broadcast_to(value_tile[80:88, :].T.astype(f32)[:, 1:2], (tile_keys, sub))

        def score(j):
            columns = slice(j * sub, (j + 1) * sub)
            found = jnp.dot(key_tile, query[0:80, columns], preferred_element_type=f32)
            if masked:
                query_ids = query[80:88, columns].astype(f32)[0:1, :]
                found = jnp.where(key_ids == query_ids, found, MASKED)
            return found

        scores = score(0)
        for j in range(count // sub):
            following = score(j + 1) if (j + 1) * sub < count else None
            columns = slice(j * sub, (j + 1) * sub)
            old = row_max[:, columns]
            if raising:
                new = jnp.maximum(old, jnp.max(scores, axis=0, keepdims=True))
                weights = jnp.exp2((scores - new) * EXP2_SCALE).astype(bf16)
                rescale = jnp.exp2((old - new) * EXP2_SCALE)
                total[:, columns] = total[:, columns] * rescale + jnp.dot(
                    value_tile, weights, preferred_element_type=f32
                )
                row_max[:, columns] = new
            else:
                weights = jnp.exp2((scores - old) * EXP2_SCALE).astype(bf16)
                total[:, columns] = total[:, columns] + jnp.dot(
                    value_tile, weights, preferred_element_type=f32
                )
                above = jnp.max(scores, axis=0, keepdims=True) - old
                excess[:, columns] = jnp.maximum(excess[:, columns], above)
            scores = following

    def every_key_block(keep_shift):
        row_max[...] = jnp.full_like(row_max, NO_MAX)
        total[...] = jnp.zeros_like(total)
        excess[...] = jnp.zeros_like(excess)

        def key_block_step(kb, started):
            low, high = limits[4 + kb, 0], limits[4 + kb, 3]
            live = jnp.logical_and(low <= q_high, high >= q_low)
            pure = q_low == q_high
            still = jnp.logical_and(
                jnp.logical_and(pure, jnp.logical_and(low == high, low == q_low)), keep_shift
            )

            @pl.when(jnp.logical_and(still, started == 0))
            def _():
                for j in range(count // sub):
                    columns = slice(j * sub, (j + 1) * sub)
                    found = jnp.dot(held_k[kb, 0:128, :], query[0:80, columns], preferred_element_type=f32)
                    row_max[:, columns] = jnp.max(found, axis=0, keepdims=True)

            @pl.when(still)
            def _():
                tile(kb, 0, count, False, False)

            @pl.when(jnp.logical_and(live, jnp.logical_not(still)))
            def _():
                def half(t, unused):
                    low, high = limits[4 + kb, 2 * t], limits[4 + kb, 2 * t + 1]

                    @pl.when(jnp.logical_and(low <= q_high, high >= q_low))
                    def _():
                        tile(kb, pl.multiple_of(t * (count // tiles), 128), count // tiles, True, True)

                    return 0

                lax.fori_loop(0, tiles, half, 0)

            return jnp.maximum(started, live.astype(jnp.int32))

        lax.fori_loop(0, 4, key_block_step, 0)

    def attempt(tried, unused):
        @pl.when(jnp.logical_or(tried == 0, jnp.max(excess[...]) > MOST_EXCESS))
        def _():
            every_key_block(tried == 0)

        return 0

    lax.fori_loop(0, 2, attempt, 0)


def store_partial(out, row_max, total):
    def split(value, parts):
        pieces = []
        for _ in range(parts):
            piece = value.astype(bf16).astype(f32)
            pieces.append(piece)
            value = value - piece
        return pieces

    rows = split(total[80:81, :], 2) + split(row_max[...], 3)
    rows.append(jnp.zeros((3, out.shape[1]), f32))
    out[0:80, :] = total[0:80, :].astype(bf16)
    out[80:88, :] = jnp.concatenate(rows, axis=0).astype(bf16)


def find_limits(ids, limits, limits_s, sem):
    count = ids.shape[1]
    lane = lax.broadcasted_iota(jnp.int32, (8, 128), 1)
    table = jnp.zeros((8, 128), f32)
    for t in range(2):
        part = ids[:, t * (count // 2) : (t + 1) * (count // 2)]
        table = jnp.where(lane == 2 * t, jnp.min(part, axis=1, keepdims=True), table)
        table = jnp.where(lane == 2 * t + 1, jnp.max(part, axis=1, keepdims=True), table)
    limits[...] = table.astype(jnp.int32)
    copy = pltpu.make_async_copy(limits, limits_s, sem)
    copy.start()
    copy.wait()


def attend_kernel(blocks, first, *refs):
    queries, refs = refs[:blocks], refs[blocks:]
    if first:
        key_values, refs = refs[:4], refs[4:]
    else:
        (held_k, held_v), refs = refs[:2], refs[2:]
    outs, refs = refs[:blocks], refs[blocks:]
    if first:
        (held_k, held_v), refs = refs[:2], refs[2:]
    query, ids, limits, limits_s, row_max, total, excess, sem = refs
    ids[...] = jnp.zeros_like(ids)
    for i in range(4):
        if first:
            held_k[i] = key_values[i][0:80, :].T
            held_v[i] = key_values[i][80:168, :]
        ids[4 + i : 5 + i, :] = held_v[i, 80:88, :].astype(f32)[1:2, :]
    for i in range(blocks):
        query[i] = queries[i][...]
        ids[i : i + 1, :] = queries[i][80:88, :].astype(f32)[0:1, :]
    find_limits(ids, limits, limits_s, sem)

    def one(i, unused):
        attend_block(query.at[i], held_k, held_v, limits_s, i, row_max, total, excess)
        for o in range(blocks):

            @pl.when(i == o)
            def _():
                store_partial(outs[o], row_max, total)

        return 0

    lax.fori_loop(0, blocks, one, 0)


def attend(queries, key_values, held=None):
    count = queries[0].shape[1]
    first = held is None
    shapes = [jax.ShapeDtypeStruct((88, count), bf16)] * len(queries)
    if first:
        shapes.append(jax.ShapeDtypeStruct((4, count, 80), bf16))
        shapes.append(jax.ShapeDtypeStruct((4, 88, count), bf16))
    operands = list(queries) + list(key_values if first else held)
    out = pl.pallas_call(
        functools.partial(attend_kernel, len(queries), first),
        out_shape=shapes,
        in_specs=[IN_VMEM] * len(operands),
        out_specs=[IN_VMEM] * len(shapes),
        scratch_shapes=[
            pltpu.VMEM((len(queries), 88, count), bf16),
            pltpu.VMEM((8, count), f32),
            pltpu.VMEM((8, 128), jnp.int32),
            pltpu.SMEM((8, 128), jnp.int32),
            pltpu.VMEM((1, count), f32),
            pltpu.VMEM((88, count), f32),
            pltpu.VMEM((1, count), f32),
            pltpu.SemaphoreType.DMA,
        ],
        compiler_params=pltpu.CompilerParams(vmem_limit_bytes=16 << 20),
        name="attend_first" if first else "attend_next",
    )(*operands)
    return list(out[: len(queries)]), list(out[len(queries) :])


def this_core():
    return lax.rem(lax.axis_index("section"), 2)


def combine_kernel(*refs):
    parts, (mine, others, whole) = refs[:4], refs[4:]
    core = this_core()
    sums, maxima = [], []
    for part in parts:
        rows = part[80:88, :].astype(f32)
        sums.append(rows[0:1, :] + rows[1:2, :])
        maxima.append((rows[2:3, :] + rows[3:4, :]) + rows[4:5, :])
    top = functools.reduce(jnp.maximum, maxima)
    factors = [jnp.exp2((m - top) * EXP2_SCALE) for m in maxima]
    inverse = 1.0 / functools.reduce(jnp.add, [w * s for w, s in zip(factors, sums)])
    mixed = functools.reduce(
        jnp.add, [part[0:80, :].astype(f32) * w for part, w in zip(parts, factors)]
    )
    whole[...] = (mixed * inverse).astype(bf16)
    half = mine.shape[1]
    mine[...] = whole[:, pl.ds(pl.multiple_of(core * half, 128), half)]
    others[...] = whole[:, pl.ds(pl.multiple_of((1 - core) * half, 128), half)]


def combine(parts):
    count = parts[0].shape[1]
    return pl.pallas_call(
        combine_kernel,
        out_shape=[jax.ShapeDtypeStruct((80, count // 2), bf16)] * 2,
        in_specs=[IN_VMEM] * 4,
        out_specs=[IN_VMEM] * 2,
        scratch_shapes=[pltpu.VMEM((80, count), bf16)],
        compiler_params=pltpu.CompilerParams(vmem_limit_bytes=6 << 20),
        name="combine",
    )(*parts)


def copies_kernel(moves, *refs):
    sources, whole, sems = refs[:-2], refs[-2], refs[-1]
    copies = []
    for i, (source, start, target, rows) in enumerate(moves):
        copies.append(
            pltpu.make_async_copy(
                sources[source].at[start : start + rows, :],
                whole.at[target : target + rows, :],
                sems.at[i],
            )
        )
        copies[-1].start()
    for copy in copies:
        copy.wait()


def place_rows(sources, moves, name, spaces=None):
    rows = sum(move[3] for move in moves)
    return pl.pallas_call(
        functools.partial(copies_kernel, moves),
        out_shape=jax.ShapeDtypeStruct((rows, sources[0].shape[1]), bf16),
        in_specs=[pl.BlockSpec(memory_space=space) for space in spaces or [pl.ANY] * len(sources)],
        out_specs=IN_VMEM,
        scratch_shapes=[pltpu.SemaphoreType.DMA((len(moves),))],
        compiler_params=pltpu.CompilerParams(vmem_limit_bytes=5 << 20),
        name=name,
    )(*sources)


def project_kernel(*refs):
    pieces = refs[:8]
    (weight, gain, shift, *projs, out_mine, out_others, normed) = refs[8:]
    width = weight.shape[1]
    count = pieces[0].shape[1]
    attended = jnp.concatenate([piece[...] for piece in pieces], axis=0)
    rows = jnp.dot(attended.T, weight[...], preferred_element_type=f32).astype(bf16).astype(f32)
    rows = rows - jnp.sum(rows, axis=1, keepdims=True) * (1.0 / width)
    spread = jnp.sum(rows * rows, axis=1, keepdims=True) * (1.0 / width)
    rows = rows * lax.rsqrt(spread + EPSILON) * gain[...] + shift[...]
    for k in range(width // 128):
        normed[k] = rows[:, k * 128 : (k + 1) * 128]
    tokens = []
    for r in range(4):
        every_fourth = pl.ds(r, count // 4, stride=4)
        tokens.append(
            jnp.concatenate(
                [normed[k, every_fourth, :].astype(bf16) for k in range(width // 128)], axis=1
            )
        )
    for out, proj in ((out_others, projs[1]), (out_mine, projs[0])):
        linear = jnp.zeros(out.shape, f32)
        for r in range(4):
            linear = linear + lax.dot_general(
                proj[:, r * width : (r + 1) * width],
                tokens[r],
                (((1,), (1,)), ((), ())),
                preferred_element_type=f32,
            )
        out[...] = linear


def project(pieces, weight, gain, shift, mine, others):
    count, width = pieces[0].shape[1], weight.shape[1]
    return pl.pallas_call(
        project_kernel,
        out_shape=[jax.ShapeDtypeStruct((mine.shape[0], count // 4), f32)] * 2,
        in_specs=[IN_VMEM] * 13,
        out_specs=[IN_VMEM] * 2,
        scratch_shapes=[pltpu.VMEM((width // 128, count, 128), f32)],
        compiler_params=pltpu.CompilerParams(vmem_limit_bytes=24 << 20),
        name="project",
    )(*pieces, weight, gain, shift, mine, others)


def finish_kernel(mine, rest, bias, out):
    core, count = this_core(), mine.shape[1]
    bias_column = jnp.broadcast_to(bias[...], (8, mine.shape[0])).T[:, 0:1]
    for place, product in ((core, mine), (1 - core, rest)):
        linear = product[...] + bias_column
        active = 0.5 * linear * (1.0 + lax.erf(linear * (0.5**0.5)))
        out[:, pl.ds(pl.multiple_of(place * count, 128), count)] = active.astype(bf16)


def finish(mine, rest, bias):
    rows, count = mine.shape
    return pl.pallas_call(
        finish_kernel,
        out_shape=jax.ShapeDtypeStruct((rows, 2 * count), bf16),
        in_specs=[IN_VMEM] * 3,
        out_specs=IN_VMEM,
        compiler_params=pltpu.CompilerParams(vmem_limit_bytes=4 << 20),
        name="finish",
    )(mine, rest, bias)


def on_device(
    queries, keys, values, segment_ids, out_weight, norm_gain, norm_bias, proj_weight, proj_bias
):
    blocks = lax.axis_size("blk")
    query_block, key_block = pack(queries.T, keys.T, values.T, segment_ids[None, :])

    sections = lax.axis_size("section")

    def swap(block, mask):
        if mask == 0:
            return block
        perm = []
        for i in range(blocks):
            for section in range(sections):
                turn = section % 2
                y, z = i // 8 ^ mask >> 3, ((i % 8 - turn) % 8 ^ mask & 7) + turn
                perm.append((i * sections + section, (y * 8 + z % 8) * sections + section))
        return lax.ppermute(block, ("blk", "section"), perm)

    def send(block, to):
        perm = []
        for x in range(4):
            for c in range(2):
                for t in range(2):
                    a, b, d = to(x, c, t)
                    perm.append(((x * 2 + c) * 2 + t, (a % 4 * 2 + b) * 2 + d))
        return lax.ppermute(block, GROUP, perm)

    def across(x, c, t):
        return x, 1 - c, t

    others = send(proj_weight.T, across)
    key_blocks = [swap(key_block, mask) for mask in KEY_PARTNERS]
    queries_at = [query_block, swap(query_block, QUERY_PARTNERS[1])]
    late_query, late_weight, others, _ = lax.optimization_barrier(
        (query_block, out_weight, others, (key_blocks, queries_at[1]))
    )
    queries_at += [swap(late_query, mask) for mask in QUERY_PARTNERS[2:]]
    far = send(late_weight, lambda x, c, t: (x, c, 1 - t))
    returned, held = attend(queries_at[:2], key_blocks)
    both = place_rows(
        [pltpu.with_memory_space_constraint(late_weight, pltpu.HBM), far],
        [(i, 0, i * HDIM, HDIM) for i in range(2)],
        "both",
        (pltpu.HBM, pl.ANY),
    )
    returned[1] = swap(returned[1], QUERY_PARTNERS[1])
    both, late_queries, held = lax.optimization_barrier((both, queries_at[2:], held))
    steps = (1, 3, 2)
    weights = [both] + [send(both, lambda x, c, t, d=d: (x + d, c, t)) for d in steps]
    late, _ = attend(late_queries, None, held)
    late, returned[1] = lax.optimization_barrier((late, returned[1]))
    returned += [swap(part, mask) for part, mask in zip(late, QUERY_PARTNERS[2:])]
    weights, late = lax.optimization_barrier((weights, late))
    half = place_rows(weights, [(i, 0, i * 160, 160) for i in range(4)], "assemble")
    returned, half = lax.optimization_barrier((returned, half))
    other_half = send(half, across)
    kept, given = combine(returned)

    pair = place_rows([kept, send(given, across)], [(i, 0, i * HDIM, HDIM) for i in range(2)], "pair")
    pieces = {(0, 0): pair, (0, 1): send(pair, lambda x, c, t: (x, c, 1 - t))}
    for e in (0, 1):
        for d in (2, 1, 3):
            pieces[d, e] = send(pieces[0, e], lambda x, c, t: (x + d, c, t))
    order = [(d, e) for d in (0,) + steps for e in (0, 1)]
    moves = [(h, i * HDIM, (2 * i + h) * HDIM, HDIM) for i in range(8) for h in range(2)]
    weight = place_rows([half, other_half], moves, "join")
    out_mine, out_others = project(
        [pieces[place] for place in order],
        weight,
        norm_gain[None, :],
        norm_bias[None, :],
        proj_weight.T,
        others,
    )
    return finish(out_mine, send(out_others, across), proj_bias[None, :]).T


def solution(mesh):
    placed = (
        P("blk", GROUP),
        P("blk", GROUP),
        P("blk", GROUP),
        P("blk"),
        P(GROUP, None),
        P(),
        P(),
        P(None, GROUP),
        P(GROUP),
    )
    return jax.shard_map(
        on_device,
        mesh=mesh,
        in_specs=placed,
        out_specs=P("blk", GROUP),
        check_vma=False,
    )
```

```python
import functools

import jax
import jax.numpy as jnp
from jax import lax
from jax.experimental import pallas as pl
from jax.experimental.pallas import tpu as pltpu
from jax.sharding import PartitionSpec as P

HDIM = 80
EPSILON = 1e-06
EXP2_SCALE = 1.4426950408889634 * HDIM ** (-0.5)
MASKED = -1e30
NO_MAX = -1e20
MOST_EXCESS = 60.0 / EXP2_SCALE
KEY_PARTNERS = (0, 1, 8, 9)
QUERY_PARTNERS = (0, 4, 10, 14)
f32, bf16 = jnp.float32, jnp.bfloat16
GROUP = ("section", "tp")
IN_VMEM = pl.BlockSpec(memory_space=pltpu.VMEM)


def pack_kernel(queries, keys, values, ids, query_block, key_block, held_ids, sems):
    count = queries.shape[1]
    moves = [
        (ids, held_ids),
        (queries, query_block.at[0:80, :]),
        (keys, key_block.at[0:80, :]),
        (values, key_block.at[80:160, :]),
    ]
    copies = [pltpu.make_async_copy(*move, sems.at[i]) for i, move in enumerate(moves)]
    for copy in copies:
        copy.start()
    copies[0].wait()
    id_row = held_ids[...].astype(f32)
    zeros = jnp.zeros((6, count), f32)
    query_block[80:88, :] = jnp.concatenate([id_row, id_row, zeros], axis=0).astype(bf16)
    key_block[160:168, :] = jnp.concatenate([jnp.ones_like(id_row), id_row, zeros], axis=0).astype(bf16)
    for copy in copies[1:]:
        copy.wait()


def pack(queries, keys, values, ids):
    count = queries.shape[1]
    return pl.pallas_call(
        pack_kernel,
        out_shape=[
            jax.ShapeDtypeStruct((88, count), bf16),
            jax.ShapeDtypeStruct((168, count), bf16),
        ],
        in_specs=[pl.BlockSpec(memory_space=pltpu.HBM)] * 4,
        out_specs=[IN_VMEM] * 2,
        scratch_shapes=[pltpu.VMEM((1, count), jnp.int32), pltpu.SemaphoreType.DMA((4,))],
        compiler_params=pltpu.CompilerParams(vmem_limit_bytes=4 << 20),
        name="pack",
    )(*(pltpu.with_memory_space_constraint(x, pltpu.HBM) for x in (queries, keys, values, ids)))


def attend_block(query, held_k, held_v, limits, which, row_max, total, excess):
    count = query.shape[1]
    tiles, sub = 2, 256
    q_low, q_high = limits[which, 0], limits[which, 3]

    def tile(kb, start, tile_keys, masked, raising):
        rows = pl.ds(start, tile_keys)
        key_tile = held_k[kb, rows, :]
        value_tile = held_v[kb, :, rows]
        if masked:
            key_ids = jnp.broadcast_to(value_tile[80:88, :].T.astype(f32)[:, 1:2], (tile_keys, sub))

        def score(j):
            columns = slice(j * sub, (j + 1) * sub)
            found = jnp.dot(key_tile, query[0:80, columns], preferred_element_type=f32)
            if masked:
                query_ids = query[80:88, columns].astype(f32)[0:1, :]
                found = jnp.where(key_ids == query_ids, found, MASKED)
            return found

        scores = score(0)
        for j in range(count // sub):
            following = score(j + 1) if (j + 1) * sub < count else None
            columns = slice(j * sub, (j + 1) * sub)
            old = row_max[:, columns]
            if raising:
                new = jnp.maximum(old, jnp.max(scores, axis=0, keepdims=True))
                weights = jnp.exp2((scores - new) * EXP2_SCALE).astype(bf16)
                rescale = jnp.exp2((old - new) * EXP2_SCALE)
                total[:, columns] = total[:, columns] * rescale + jnp.dot(
                    value_tile, weights, preferred_element_type=f32
                )
                row_max[:, columns] = new
            else:
                weights = jnp.exp2((scores - old) * EXP2_SCALE).astype(bf16)
                total[:, columns] = total[:, columns] + jnp.dot(
                    value_tile, weights, preferred_element_type=f32
                )
                above = jnp.max(scores, axis=0, keepdims=True) - old
                excess[:, columns] = jnp.maximum(excess[:, columns], above)
            scores = following

    def every_key_block(keep_shift):
        row_max[...] = jnp.full_like(row_max, NO_MAX)
        total[...] = jnp.zeros_like(total)
        excess[...] = jnp.zeros_like(excess)

        def key_block_step(kb, started):
            low, high = limits[4 + kb, 0], limits[4 + kb, 3]
            live = jnp.logical_and(low <= q_high, high >= q_low)
            pure = q_low == q_high
            still = jnp.logical_and(
                jnp.logical_and(pure, jnp.logical_and(low == high, low == q_low)), keep_shift
            )

            @pl.when(jnp.logical_and(still, started == 0))
            def _():
                for j in range(count // sub):
                    columns = slice(j * sub, (j + 1) * sub)
                    found = jnp.dot(held_k[kb, 0:128, :], query[0:80, columns], preferred_element_type=f32)
                    row_max[:, columns] = jnp.max(found, axis=0, keepdims=True)

            @pl.when(still)
            def _():
                tile(kb, 0, count, False, False)

            @pl.when(jnp.logical_and(live, jnp.logical_not(still)))
            def _():
                def half(t, unused):
                    low, high = limits[4 + kb, 2 * t], limits[4 + kb, 2 * t + 1]

                    @pl.when(jnp.logical_and(low <= q_high, high >= q_low))
                    def _():
                        tile(kb, pl.multiple_of(t * (count // tiles), 128), count // tiles, True, True)

                    return 0

                lax.fori_loop(0, tiles, half, 0)

            return jnp.maximum(started, live.astype(jnp.int32))

        lax.fori_loop(0, 4, key_block_step, 0)

    def attempt(tried, unused):
        @pl.when(jnp.logical_or(tried == 0, jnp.max(excess[...]) > MOST_EXCESS))
        def _():
            every_key_block(tried == 0)

        return 0

    lax.fori_loop(0, 2, attempt, 0)


def store_partial(out, row_max, total):
    def split(value, parts):
        pieces = []
        for _ in range(parts):
            piece = value.astype(bf16).astype(f32)
            pieces.append(piece)
            value = value - piece
        return pieces

    rows = split(total[80:81, :], 2) + split(row_max[...], 3)
    rows.append(jnp.zeros((3, out.shape[1]), f32))
    out[0:80, :] = total[0:80, :].astype(bf16)
    out[80:88, :] = jnp.concatenate(rows, axis=0).astype(bf16)


def find_limits(ids, limits, limits_s, sem):
    count = ids.shape[1]
    lane = lax.broadcasted_iota(jnp.int32, (8, 128), 1)
    table = jnp.zeros((8, 128), f32)
    for t in range(2):
        part = ids[:, t * (count // 2) : (t + 1) * (count // 2)]
        table = jnp.where(lane == 2 * t, jnp.min(part, axis=1, keepdims=True), table)
        table = jnp.where(lane == 2 * t + 1, jnp.max(part, axis=1, keepdims=True), table)
    limits[...] = table.astype(jnp.int32)
    copy = pltpu.make_async_copy(limits, limits_s, sem)
    copy.start()
    copy.wait()


def attend_kernel(blocks, first, *refs):
    queries, refs = refs[:blocks], refs[blocks:]
    if first:
        key_values, refs = refs[:4], refs[4:]
    else:
        (held_k, held_v), refs = refs[:2], refs[2:]
    outs, refs = refs[:blocks], refs[blocks:]
    if first:
        (held_k, held_v), refs = refs[:2], refs[2:]
    query, ids, limits, limits_s, row_max, total, excess, sem = refs
    ids[...] = jnp.zeros_like(ids)
    for i in range(4):
        if first:
            held_k[i] = key_values[i][0:80, :].T
            held_v[i] = key_values[i][80:168, :]
        ids[4 + i : 5 + i, :] = held_v[i, 80:88, :].astype(f32)[1:2, :]
    for i in range(blocks):
        query[i] = queries[i][...]
        ids[i : i + 1, :] = queries[i][80:88, :].astype(f32)[0:1, :]
    find_limits(ids, limits, limits_s, sem)

    def one(i, unused):
        attend_block(query.at[i], held_k, held_v, limits_s, i, row_max, total, excess)
        for o in range(blocks):

            @pl.when(i == o)
            def _():
                store_partial(outs[o], row_max, total)

        return 0

    lax.fori_loop(0, blocks, one, 0)


def attend(queries, key_values, held=None):
    count = queries[0].shape[1]
    first = held is None
    shapes = [jax.ShapeDtypeStruct((88, count), bf16)] * len(queries)
    if first:
        shapes.append(jax.ShapeDtypeStruct((4, count, 80), bf16))
        shapes.append(jax.ShapeDtypeStruct((4, 88, count), bf16))
    operands = list(queries) + list(key_values if first else held)
    out = pl.pallas_call(
        functools.partial(attend_kernel, len(queries), first),
        out_shape=shapes,
        in_specs=[IN_VMEM] * len(operands),
        out_specs=[IN_VMEM] * len(shapes),
        scratch_shapes=[
            pltpu.VMEM((len(queries), 88, count), bf16),
            pltpu.VMEM((8, count), f32),
            pltpu.VMEM((8, 128), jnp.int32),
            pltpu.SMEM((8, 128), jnp.int32),
            pltpu.VMEM((1, count), f32),
            pltpu.VMEM((88, count), f32),
            pltpu.VMEM((1, count), f32),
            pltpu.SemaphoreType.DMA,
        ],
        compiler_params=pltpu.CompilerParams(vmem_limit_bytes=16 << 20),
        name="attend_first" if first else "attend_next",
    )(*operands)
    return list(out[: len(queries)]), list(out[len(queries) :])


def this_core():
    return lax.rem(lax.axis_index("section"), 2)


def combine_kernel(*refs):
    parts, (mine, others, whole) = refs[:4], refs[4:]
    core = this_core()
    sums, maxima = [], []
    for part in parts:
        rows = part[80:88, :].astype(f32)
        sums.append(rows[0:1, :] + rows[1:2, :])
        maxima.append((rows[2:3, :] + rows[3:4, :]) + rows[4:5, :])
    top = functools.reduce(jnp.maximum, maxima)
    factors = [jnp.exp2((m - top) * EXP2_SCALE) for m in maxima]
    inverse = 1.0 / functools.reduce(jnp.add, [w * s for w, s in zip(factors, sums)])
    mixed = functools.reduce(
        jnp.add, [part[0:80, :].astype(f32) * w for part, w in zip(parts, factors)]
    )
    whole[...] = (mixed * inverse).astype(bf16)
    half = mine.shape[1]
    mine[...] = whole[:, pl.ds(pl.multiple_of(core * half, 128), half)]
    others[...] = whole[:, pl.ds(pl.multiple_of((1 - core) * half, 128), half)]


def combine(parts):
    count = parts[0].shape[1]
    return pl.pallas_call(
        combine_kernel,
        out_shape=[jax.ShapeDtypeStruct((80, count // 2), bf16)] * 2,
        in_specs=[IN_VMEM] * 4,
        out_specs=[IN_VMEM] * 2,
        scratch_shapes=[pltpu.VMEM((80, count), bf16)],
        compiler_params=pltpu.CompilerParams(vmem_limit_bytes=6 << 20),
        name="combine",
    )(*parts)


def copies_kernel(moves, *refs):
    sources, whole, sems = refs[:-2], refs[-2], refs[-1]
    copies = []
    for i, (source, start, target, rows) in enumerate(moves):
        copies.append(
            pltpu.make_async_copy(
                sources[source].at[start : start + rows, :],
                whole.at[target : target + rows, :],
                sems.at[i],
            )
        )
        copies[-1].start()
    for copy in copies:
        copy.wait()


def place_rows(sources, moves, name, spaces=None):
    rows = sum(move[3] for move in moves)
    return pl.pallas_call(
        functools.partial(copies_kernel, moves),
        out_shape=jax.ShapeDtypeStruct((rows, sources[0].shape[1]), bf16),
        in_specs=[pl.BlockSpec(memory_space=space) for space in spaces or [pl.ANY] * len(sources)],
        out_specs=IN_VMEM,
        scratch_shapes=[pltpu.SemaphoreType.DMA((len(moves),))],
        compiler_params=pltpu.CompilerParams(vmem_limit_bytes=5 << 20),
        name=name,
    )(*sources)


def project_kernel(*refs):
    pieces = refs[:8]
    (weight, gain, shift, *projs, out_mine, out_others, normed) = refs[8:]
    width = weight.shape[1]
    count = pieces[0].shape[1]
    attended = jnp.concatenate([piece[...] for piece in pieces], axis=0)
    rows = jnp.dot(attended.T, weight[...], preferred_element_type=f32).astype(bf16).astype(f32)
    rows = rows - jnp.sum(rows, axis=1, keepdims=True) * (1.0 / width)
    spread = jnp.sum(rows * rows, axis=1, keepdims=True) * (1.0 / width)
    rows = rows * lax.rsqrt(spread + EPSILON) * gain[...] + shift[...]
    for k in range(width // 128):
        normed[k] = rows[:, k * 128 : (k + 1) * 128]
    tokens = []
    for r in range(4):
        every_fourth = pl.ds(r, count // 4, stride=4)
        tokens.append(
            jnp.concatenate(
                [normed[k, every_fourth, :].astype(bf16) for k in range(width // 128)], axis=1
            )
        )
    for out, proj in ((out_others, projs[1]), (out_mine, projs[0])):
        linear = jnp.zeros(out.shape, f32)
        for r in range(4):
            linear = linear + lax.dot_general(
                proj[:, r * width : (r + 1) * width],
                tokens[r],
                (((1,), (1,)), ((), ())),
                preferred_element_type=f32,
            )
        out[...] = linear


def project(pieces, weight, gain, shift, mine, others):
    count, width = pieces[0].shape[1], weight.shape[1]
    return pl.pallas_call(
        project_kernel,
        out_shape=[jax.ShapeDtypeStruct((mine.shape[0], count // 4), f32)] * 2,
        in_specs=[IN_VMEM] * 13,
        out_specs=[IN_VMEM] * 2,
        scratch_shapes=[pltpu.VMEM((width // 128, count, 128), f32)],
        compiler_params=pltpu.CompilerParams(vmem_limit_bytes=24 << 20),
        name="project",
    )(*pieces, weight, gain, shift, mine, others)


def finish_kernel(mine, rest, bias, out):
    core, count = this_core(), mine.shape[1]
    bias_column = jnp.broadcast_to(bias[...], (8, mine.shape[0])).T[:, 0:1]
    for place, product in ((core, mine), (1 - core, rest)):
        linear = product[...] + bias_column
        active = 0.5 * linear * (1.0 + lax.erf(linear * (0.5**0.5)))
        out[:, pl.ds(pl.multiple_of(place * count, 128), count)] = active.astype(bf16)


def finish(mine, rest, bias):
    rows, count = mine.shape
    return pl.pallas_call(
        finish_kernel,
        out_shape=jax.ShapeDtypeStruct((rows, 2 * count), bf16),
        in_specs=[IN_VMEM] * 3,
        out_specs=IN_VMEM,
        compiler_params=pltpu.CompilerParams(vmem_limit_bytes=4 << 20),
        name="finish",
    )(mine, rest, bias)


def on_device(
    queries, keys, values, segment_ids, out_weight, norm_gain, norm_bias, proj_weight, proj_bias
):
    blocks = lax.axis_size("blk")
    query_block, key_block = pack(queries.T, keys.T, values.T, segment_ids[None, :])

    sections = lax.axis_size("section")

    def swap(block, mask):
        if mask == 0:
            return block
        perm = []
        for i in range(blocks):
            for section in range(sections):
                turn = section % 2
                y, z = i // 8 ^ mask >> 3, ((i % 8 - turn) % 8 ^ mask & 7) + turn
                perm.append((i * sections + section, (y * 8 + z % 8) * sections + section))
        return lax.ppermute(block, ("blk", "section"), perm)

    def send(block, to):
        perm = []
        for x in range(4):
            for c in range(2):
                for t in range(2):
                    a, b, d = to(x, c, t)
                    perm.append(((x * 2 + c) * 2 + t, (a % 4 * 2 + b) * 2 + d))
        return lax.ppermute(block, GROUP, perm)

    def across(x, c, t):
        return x, 1 - c, t

    others = send(proj_weight.T, across)
    key_blocks = [swap(key_block, mask) for mask in KEY_PARTNERS]
    queries_at = [query_block, swap(query_block, QUERY_PARTNERS[1])]
    late_query, late_weight, others, _ = lax.optimization_barrier(
        (query_block, out_weight, others, (key_blocks, queries_at[1]))
    )
    queries_at += [swap(late_query, mask) for mask in QUERY_PARTNERS[2:]]
    far = send(late_weight, lambda x, c, t: (x, c, 1 - t))
    (first,), held = attend([queries_at[1]], key_blocks)
    both = place_rows(
        [pltpu.with_memory_space_constraint(late_weight, pltpu.HBM), far],
        [(i, 0, i * HDIM, HDIM) for i in range(2)],
        "both",
        (pltpu.HBM, pl.ANY),
    )
    first = swap(first, QUERY_PARTNERS[1])
    both, late_queries, held = lax.optimization_barrier((both, queries_at[2:], held))
    steps = (1, 3, 2)
    weights = [both] + [send(both, lambda x, c, t, d=d: (x + d, c, t)) for d in steps]
    late, _ = attend(late_queries, None, held)
    late, first = lax.optimization_barrier((late, first))
    own_query, _ = lax.optimization_barrier((query_block, late))
    (own,), _ = attend([own_query], None, held)
    returned = [own, first] + [swap(part, mask) for part, mask in zip(late, QUERY_PARTNERS[2:])]
    weights, returned[0] = lax.optimization_barrier((weights, own))
    half = place_rows(weights, [(i, 0, i * 160, 160) for i in range(4)], "assemble")
    returned, half = lax.optimization_barrier((returned, half))
    other_half = send(half, across)
    kept, given = combine(returned)

    pair = place_rows([kept, send(given, across)], [(i, 0, i * HDIM, HDIM) for i in range(2)], "pair")
    pieces = {(0, 0): pair, (0, 1): send(pair, lambda x, c, t: (x, c, 1 - t))}
    for e in (0, 1):
        for d in (2, 1, 3):
            pieces[d, e] = send(pieces[0, e], lambda x, c, t: (x + d, c, t))
    order = [(d, e) for d in (0,) + steps for e in (0, 1)]
    moves = [(h, i * HDIM, (2 * i + h) * HDIM, HDIM) for i in range(8) for h in range(2)]
    weight = place_rows([half, other_half], moves, "join")
    out_mine, out_others = project(
        [pieces[place] for place in order],
        weight,
        norm_gain[None, :],
        norm_bias[None, :],
        proj_weight.T,
        others,
    )
    return finish(out_mine, send(out_others, across), proj_bias[None, :]).T


def solution(mesh):
    placed = (
        P("blk", GROUP),
        P("blk", GROUP),
        P("blk", GROUP),
        P("blk"),
        P(GROUP, None),
        P(),
        P(),
        P(None, GROUP),
        P(GROUP),
    )
    return jax.shard_map(
        on_device,
        mesh=mesh,
        in_specs=placed,
        out_specs=P("blk", GROUP),
        check_vma=False,
    )
```

```python
import functools

import jax
import jax.numpy as jnp
from jax import lax
from jax.experimental import pallas as pl
from jax.experimental.pallas import tpu as pltpu
from jax.sharding import PartitionSpec as P

HDIM = 80
EPSILON = 1e-06
EXP2_SCALE = 1.4426950408889634 * HDIM ** (-0.5)
MASKED = -1e30
NO_MAX = -1e20
MOST_EXCESS = 60.0 / EXP2_SCALE
KEY_PARTNERS = (0, 1, 8, 9)
QUERY_PARTNERS = (0, 4, 10, 14)
f32, bf16 = jnp.float32, jnp.bfloat16
GROUP = ("section", "tp")
IN_VMEM = pl.BlockSpec(memory_space=pltpu.VMEM)


def pack_kernel(queries, keys, values, ids, query_block, key_block, held_ids, sems):
    count = queries.shape[1]
    moves = [
        (ids, held_ids),
        (queries, query_block.at[0:80, :]),
        (keys, key_block.at[0:80, :]),
        (values, key_block.at[80:160, :]),
    ]
    copies = [pltpu.make_async_copy(*move, sems.at[i]) for i, move in enumerate(moves)]
    for copy in copies:
        copy.start()
    copies[0].wait()
    id_row = held_ids[...].astype(f32)
    zeros = jnp.zeros((6, count), f32)
    query_block[80:88, :] = jnp.concatenate([id_row, id_row, zeros], axis=0).astype(bf16)
    key_block[160:168, :] = jnp.concatenate([jnp.ones_like(id_row), id_row, zeros], axis=0).astype(bf16)
    for copy in copies[1:]:
        copy.wait()


def pack(queries, keys, values, ids):
    count = queries.shape[1]
    return pl.pallas_call(
        pack_kernel,
        out_shape=[
            jax.ShapeDtypeStruct((88, count), bf16),
            jax.ShapeDtypeStruct((168, count), bf16),
        ],
        in_specs=[pl.BlockSpec(memory_space=pltpu.HBM)] * 4,
        out_specs=[IN_VMEM] * 2,
        scratch_shapes=[pltpu.VMEM((1, count), jnp.int32), pltpu.SemaphoreType.DMA((4,))],
        compiler_params=pltpu.CompilerParams(vmem_limit_bytes=4 << 20),
        name="pack",
    )(*(pltpu.with_memory_space_constraint(x, pltpu.HBM) for x in (queries, keys, values, ids)))


def attend_block(query, held_k, held_v, limits, which, row_max, total, excess):
    count = query.shape[1]
    tiles, sub = 2, 256
    q_low, q_high = limits[which, 0], limits[which, 3]

    def tile(kb, start, tile_keys, masked, raising, low=None, high=None):
        rows = pl.ds(start, tile_keys)
        key_tile = held_k[kb, rows, :]
        value_tile = held_v[kb, :, rows]
        if masked:
            key_ids = jnp.broadcast_to(value_tile[80:88, :].T.astype(f32)[:, 1:2], (tile_keys, sub))

        def score(j):
            columns = slice(j * sub, (j + 1) * sub)
            found = jnp.dot(key_tile, query[0:80, columns], preferred_element_type=f32)
            if masked:
                query_ids = query[80:88, columns].astype(f32)[0:1, :]
                found = jnp.where(key_ids == query_ids, found, MASKED)
            return found

        def part(j, scores):
            columns = slice(j * sub, (j + 1) * sub)
            old = row_max[:, columns]
            if raising:
                new = jnp.maximum(old, jnp.max(scores, axis=0, keepdims=True))
                weights = jnp.exp2((scores - new) * EXP2_SCALE).astype(bf16)
                rescale = jnp.exp2((old - new) * EXP2_SCALE)
                total[:, columns] = total[:, columns] * rescale + jnp.dot(
                    value_tile, weights, preferred_element_type=f32
                )
                row_max[:, columns] = new
            else:
                weights = jnp.exp2((scores - old) * EXP2_SCALE).astype(bf16)
                total[:, columns] = total[:, columns] + jnp.dot(
                    value_tile, weights, preferred_element_type=f32
                )
                above = jnp.max(scores, axis=0, keepdims=True) - old
                excess[:, columns] = jnp.maximum(excess[:, columns], above)

        if low is not None:
            for j in range(count // sub):
                overlaps = jnp.logical_and(
                    low <= limits[which, 5 + 2 * j], high >= limits[which, 4 + 2 * j]
                )

                @pl.when(overlaps)
                def _():
                    part(j, score(j))

            return
        scores = score(0)
        for j in range(count // sub):
            following = score(j + 1) if (j + 1) * sub < count else None
            part(j, scores)
            scores = following

    def every_key_block(keep_shift):
        row_max[...] = jnp.full_like(row_max, NO_MAX)
        total[...] = jnp.zeros_like(total)
        excess[...] = jnp.zeros_like(excess)

        def key_block_step(kb, started):
            low, high = limits[4 + kb, 0], limits[4 + kb, 3]
            live = jnp.logical_and(low <= q_high, high >= q_low)
            pure = q_low == q_high
            still = jnp.logical_and(
                jnp.logical_and(pure, jnp.logical_and(low == high, low == q_low)), keep_shift
            )

            @pl.when(jnp.logical_and(still, started == 0))
            def _():
                for j in range(count // sub):
                    columns = slice(j * sub, (j + 1) * sub)
                    found = jnp.dot(held_k[kb, 0:128, :], query[0:80, columns], preferred_element_type=f32)
                    row_max[:, columns] = jnp.max(found, axis=0, keepdims=True)

            @pl.when(still)
            def _():
                tile(kb, 0, count, False, False)

            @pl.when(jnp.logical_and(live, jnp.logical_not(still)))
            def _():
                def half(t, unused):
                    low, high = limits[4 + kb, 2 * t], limits[4 + kb, 2 * t + 1]

                    touches = jnp.logical_and(low <= q_high, high >= q_low)
                    begin = pl.multiple_of(t * (count // tiles), 128)

                    @pl.when(jnp.logical_and(touches, pure))
                    def _():
                        tile(kb, begin, count // tiles, True, True)

                    @pl.when(jnp.logical_and(touches, jnp.logical_not(pure)))
                    def _():
                        tile(kb, begin, count // tiles, True, True, low, high)

                    return 0

                lax.fori_loop(0, tiles, half, 0)

            return jnp.maximum(started, live.astype(jnp.int32))

        lax.fori_loop(0, 4, key_block_step, 0)

    def attempt(tried, unused):
        @pl.when(jnp.logical_or(tried == 0, jnp.max(excess[...]) > MOST_EXCESS))
        def _():
            every_key_block(tried == 0)

        return 0

    lax.fori_loop(0, 2, attempt, 0)


def store_partial(out, row_max, total):
    def split(value, parts):
        pieces = []
        for _ in range(parts):
            piece = value.astype(bf16).astype(f32)
            pieces.append(piece)
            value = value - piece
        return pieces

    rows = split(total[80:81, :], 2) + split(row_max[...], 3)
    rows.append(jnp.zeros((3, out.shape[1]), f32))
    out[0:80, :] = total[0:80, :].astype(bf16)
    out[80:88, :] = jnp.concatenate(rows, axis=0).astype(bf16)


def find_limits(ids, limits, limits_s, sem):
    count = ids.shape[1]
    lane = lax.broadcasted_iota(jnp.int32, (8, 128), 1)
    table = jnp.zeros((8, 128), f32)
    for t in range(2):
        part = ids[:, t * (count // 2) : (t + 1) * (count // 2)]
        table = jnp.where(lane == 2 * t, jnp.min(part, axis=1, keepdims=True), table)
        table = jnp.where(lane == 2 * t + 1, jnp.max(part, axis=1, keepdims=True), table)
    for t in range(4):
        part = ids[:, t * (count // 4) : (t + 1) * (count // 4)]
        table = jnp.where(lane == 4 + 2 * t, jnp.min(part, axis=1, keepdims=True), table)
        table = jnp.where(lane == 5 + 2 * t, jnp.max(part, axis=1, keepdims=True), table)
    limits[...] = table.astype(jnp.int32)
    copy = pltpu.make_async_copy(limits, limits_s, sem)
    copy.start()
    copy.wait()


def attend_kernel(blocks, first, *refs):
    queries, refs = refs[:blocks], refs[blocks:]
    if first:
        key_values, refs = refs[:4], refs[4:]
    else:
        (held_k, held_v), refs = refs[:2], refs[2:]
    outs, refs = refs[:blocks], refs[blocks:]
    if first:
        (held_k, held_v), refs = refs[:2], refs[2:]
    query, ids, limits, limits_s, row_max, total, excess, sem = refs
    ids[...] = jnp.zeros_like(ids)
    for i in range(4):
        if first:
            held_k[i] = key_values[i][0:80, :].T
            held_v[i] = key_values[i][80:168, :]
        ids[4 + i : 5 + i, :] = held_v[i, 80:88, :].astype(f32)[1:2, :]
    for i in range(blocks):
        query[i] = queries[i][...]
        ids[i : i + 1, :] = queries[i][80:88, :].astype(f32)[0:1, :]
    find_limits(ids, limits, limits_s, sem)

    def one(i, unused):
        attend_block(query.at[i], held_k, held_v, limits_s, i, row_max, total, excess)
        for o in range(blocks):

            @pl.when(i == o)
            def _():
                store_partial(outs[o], row_max, total)

        return 0

    lax.fori_loop(0, blocks, one, 0)


def attend(queries, key_values, held=None):
    count = queries[0].shape[1]
    first = held is None
    shapes = [jax.ShapeDtypeStruct((88, count), bf16)] * len(queries)
    if first:
        shapes.append(jax.ShapeDtypeStruct((4, count, 80), bf16))
        shapes.append(jax.ShapeDtypeStruct((4, 88, count), bf16))
    operands = list(queries) + list(key_values if first else held)
    out = pl.pallas_call(
        functools.partial(attend_kernel, len(queries), first),
        out_shape=shapes,
        in_specs=[IN_VMEM] * len(operands),
        out_specs=[IN_VMEM] * len(shapes),
        scratch_shapes=[
            pltpu.VMEM((len(queries), 88, count), bf16),
            pltpu.VMEM((8, count), f32),
            pltpu.VMEM((8, 128), jnp.int32),
            pltpu.SMEM((8, 128), jnp.int32),
            pltpu.VMEM((1, count), f32),
            pltpu.VMEM((88, count), f32),
            pltpu.VMEM((1, count), f32),
            pltpu.SemaphoreType.DMA,
        ],
        compiler_params=pltpu.CompilerParams(vmem_limit_bytes=16 << 20),
        name="attend_first" if first else "attend_next",
    )(*operands)
    return list(out[: len(queries)]), list(out[len(queries) :])


def this_core():
    return lax.rem(lax.axis_index("section"), 2)


def combine_kernel(*refs):
    parts, (mine, others, whole) = refs[:4], refs[4:]
    core = this_core()
    sums, maxima = [], []
    for part in parts:
        rows = part[80:88, :].astype(f32)
        sums.append(rows[0:1, :] + rows[1:2, :])
        maxima.append((rows[2:3, :] + rows[3:4, :]) + rows[4:5, :])
    top = functools.reduce(jnp.maximum, maxima)
    factors = [jnp.exp2((m - top) * EXP2_SCALE) for m in maxima]
    inverse = 1.0 / functools.reduce(jnp.add, [w * s for w, s in zip(factors, sums)])
    mixed = functools.reduce(
        jnp.add, [part[0:80, :].astype(f32) * w for part, w in zip(parts, factors)]
    )
    whole[...] = (mixed * inverse).astype(bf16)
    half = mine.shape[1]
    mine[...] = whole[:, pl.ds(pl.multiple_of(core * half, 128), half)]
    others[...] = whole[:, pl.ds(pl.multiple_of((1 - core) * half, 128), half)]


def combine(parts):
    count = parts[0].shape[1]
    return pl.pallas_call(
        combine_kernel,
        out_shape=[jax.ShapeDtypeStruct((80, count // 2), bf16)] * 2,
        in_specs=[IN_VMEM] * 4,
        out_specs=[IN_VMEM] * 2,
        scratch_shapes=[pltpu.VMEM((80, count), bf16)],
        compiler_params=pltpu.CompilerParams(vmem_limit_bytes=6 << 20),
        name="combine",
    )(*parts)


def copies_kernel(moves, *refs):
    sources, whole, sems = refs[:-2], refs[-2], refs[-1]
    copies = []
    for i, (source, start, target, rows) in enumerate(moves):
        copies.append(
            pltpu.make_async_copy(
                sources[source].at[start : start + rows, :],
                whole.at[target : target + rows, :],
                sems.at[i],
            )
        )
        copies[-1].start()
    for copy in copies:
        copy.wait()


def place_rows(sources, moves, name, spaces=None):
    rows = sum(move[3] for move in moves)
    return pl.pallas_call(
        functools.partial(copies_kernel, moves),
        out_shape=jax.ShapeDtypeStruct((rows, sources[0].shape[1]), bf16),
        in_specs=[pl.BlockSpec(memory_space=space) for space in spaces or [pl.ANY] * len(sources)],
        out_specs=IN_VMEM,
        scratch_shapes=[pltpu.SemaphoreType.DMA((len(moves),))],
        compiler_params=pltpu.CompilerParams(vmem_limit_bytes=5 << 20),
        name=name,
    )(*sources)


def project_kernel(*refs):
    pieces = refs[:8]
    (weight, gain, shift, *projs, out_mine, out_others, normed) = refs[8:]
    width = weight.shape[1]
    count = pieces[0].shape[1]
    attended = jnp.concatenate([piece[...] for piece in pieces], axis=0)
    rows = jnp.dot(attended.T, weight[...], preferred_element_type=f32).astype(bf16).astype(f32)
    rows = rows - jnp.sum(rows, axis=1, keepdims=True) * (1.0 / width)
    spread = jnp.sum(rows * rows, axis=1, keepdims=True) * (1.0 / width)
    rows = rows * lax.rsqrt(spread + EPSILON) * gain[...] + shift[...]
    for k in range(width // 128):
        normed[k] = rows[:, k * 128 : (k + 1) * 128]
    tokens = []
    for r in range(4):
        every_fourth = pl.ds(r, count // 4, stride=4)
        tokens.append(
            jnp.concatenate(
                [normed[k, every_fourth, :].astype(bf16) for k in range(width // 128)], axis=1
            )
        )
    for out, proj in ((out_others, projs[1]), (out_mine, projs[0])):
        linear = jnp.zeros(out.shape, f32)
        for r in range(4):
            linear = linear + lax.dot_general(
                proj[:, r * width : (r + 1) * width],
                tokens[r],
                (((1,), (1,)), ((), ())),
                preferred_element_type=f32,
            )
        out[...] = linear


def project(pieces, weight, gain, shift, mine, others):
    count, width = pieces[0].shape[1], weight.shape[1]
    return pl.pallas_call(
        project_kernel,
        out_shape=[jax.ShapeDtypeStruct((mine.shape[0], count // 4), f32)] * 2,
        in_specs=[IN_VMEM] * 13,
        out_specs=[IN_VMEM] * 2,
        scratch_shapes=[pltpu.VMEM((width // 128, count, 128), f32)],
        compiler_params=pltpu.CompilerParams(vmem_limit_bytes=24 << 20),
        name="project",
    )(*pieces, weight, gain, shift, mine, others)


def finish_kernel(mine, rest, bias, out):
    core, count = this_core(), mine.shape[1]
    bias_column = jnp.broadcast_to(bias[...], (8, mine.shape[0])).T[:, 0:1]
    for place, product in ((core, mine), (1 - core, rest)):
        linear = product[...] + bias_column
        active = 0.5 * linear * (1.0 + lax.erf(linear * (0.5**0.5)))
        out[:, pl.ds(pl.multiple_of(place * count, 128), count)] = active.astype(bf16)


def finish(mine, rest, bias):
    rows, count = mine.shape
    return pl.pallas_call(
        finish_kernel,
        out_shape=jax.ShapeDtypeStruct((rows, 2 * count), bf16),
        in_specs=[IN_VMEM] * 3,
        out_specs=IN_VMEM,
        compiler_params=pltpu.CompilerParams(vmem_limit_bytes=4 << 20),
        name="finish",
    )(mine, rest, bias)


def on_device(
    queries, keys, values, segment_ids, out_weight, norm_gain, norm_bias, proj_weight, proj_bias
):
    blocks = lax.axis_size("blk")
    query_block, key_block = pack(queries.T, keys.T, values.T, segment_ids[None, :])

    sections = lax.axis_size("section")

    def swap(block, mask):
        if mask == 0:
            return block
        perm = []
        for i in range(blocks):
            for section in range(sections):
                turn = section % 2
                y, z = i // 8 ^ mask >> 3, ((i % 8 - turn) % 8 ^ mask & 7) + turn
                perm.append((i * sections + section, (y * 8 + z % 8) * sections + section))
        return lax.ppermute(block, ("blk", "section"), perm)

    def send(block, to):
        perm = []
        for x in range(4):
            for c in range(2):
                for t in range(2):
                    a, b, d = to(x, c, t)
                    perm.append(((x * 2 + c) * 2 + t, (a % 4 * 2 + b) * 2 + d))
        return lax.ppermute(block, GROUP, perm)

    def across(x, c, t):
        return x, 1 - c, t

    others = send(proj_weight.T, across)
    key_blocks = [swap(key_block, mask) for mask in KEY_PARTNERS]
    queries_at = [query_block, swap(query_block, QUERY_PARTNERS[1])]
    late_query, late_weight, others, _ = lax.optimization_barrier(
        (query_block, out_weight, others, (key_blocks, queries_at[1]))
    )
    queries_at += [swap(late_query, mask) for mask in QUERY_PARTNERS[2:]]
    far = send(late_weight, lambda x, c, t: (x, c, 1 - t))
    (first,), held = attend([queries_at[1]], key_blocks)
    both = place_rows(
        [pltpu.with_memory_space_constraint(late_weight, pltpu.HBM), far],
        [(i, 0, i * HDIM, HDIM) for i in range(2)],
        "both",
        (pltpu.HBM, pl.ANY),
    )
    first = swap(first, QUERY_PARTNERS[1])
    both, late_queries, held = lax.optimization_barrier((both, queries_at[2:], held))
    steps = (1, 3, 2)
    weights = [both] + [send(both, lambda x, c, t, d=d: (x + d, c, t)) for d in steps]
    late, _ = attend(late_queries, None, held)
    late, first = lax.optimization_barrier((late, first))
    own_query, _ = lax.optimization_barrier((query_block, late))
    (own,), _ = attend([own_query], None, held)
    returned = [own, first] + [swap(part, mask) for part, mask in zip(late, QUERY_PARTNERS[2:])]
    weights, returned[0] = lax.optimization_barrier((weights, own))
    half = place_rows(weights, [(i, 0, i * 160, 160) for i in range(4)], "assemble")
    returned, half = lax.optimization_barrier((returned, half))
    other_half = send(half, across)
    kept, given = combine(returned)

    pair = place_rows([kept, send(given, across)], [(i, 0, i * HDIM, HDIM) for i in range(2)], "pair")
    pieces = {(0, 0): pair, (0, 1): send(pair, lambda x, c, t: (x, c, 1 - t))}
    for e in (0, 1):
        for d in (2, 1, 3):
            pieces[d, e] = send(pieces[0, e], lambda x, c, t: (x + d, c, t))
    order = [(d, e) for d in (0,) + steps for e in (0, 1)]
    moves = [(h, i * HDIM, (2 * i + h) * HDIM, HDIM) for i in range(8) for h in range(2)]
    weight = place_rows([half, other_half], moves, "join")
    out_mine, out_others = project(
        [pieces[place] for place in order],
        weight,
        norm_gain[None, :],
        norm_bias[None, :],
        proj_weight.T,
        others,
    )
    return finish(out_mine, send(out_others, across), proj_bias[None, :]).T


def solution(mesh):
    placed = (
        P("blk", GROUP),
        P("blk", GROUP),
        P("blk", GROUP),
        P("blk"),
        P(GROUP, None),
        P(),
        P(),
        P(None, GROUP),
        P(GROUP),
    )
    return jax.shard_map(
        on_device,
        mesh=mesh,
        in_specs=placed,
        out_specs=P("blk", GROUP),
        check_vma=False,
    )
```

```python
import functools

import jax
import jax.numpy as jnp
from jax import lax
from jax.experimental import pallas as pl
from jax.experimental.pallas import tpu as pltpu
from jax.sharding import PartitionSpec as P

HDIM = 80
EPSILON = 1e-06
EXP2_SCALE = 1.4426950408889634 * HDIM ** (-0.5)
MASKED = -1e30
NO_MAX = -1e20
MOST_EXCESS = 60.0 / EXP2_SCALE
KEY_PARTNERS = (0, 1, 8, 9)
QUERY_PARTNERS = (0, 4, 10, 14)
f32, bf16 = jnp.float32, jnp.bfloat16
GROUP = ("section", "tp")
IN_VMEM = pl.BlockSpec(memory_space=pltpu.VMEM)


def pack_kernel(queries, keys, values, ids, query_block, key_block, held_ids, sems):
    count = queries.shape[1]
    moves = [
        (ids, held_ids),
        (queries, query_block.at[0:80, :]),
        (keys, key_block.at[0:80, :]),
        (values, key_block.at[80:160, :]),
    ]
    copies = [pltpu.make_async_copy(*move, sems.at[i]) for i, move in enumerate(moves)]
    for copy in copies:
        copy.start()
    copies[0].wait()
    id_row = held_ids[...].astype(f32)
    zeros = jnp.zeros((6, count), f32)
    query_block[80:88, :] = jnp.concatenate([id_row, id_row, zeros], axis=0).astype(bf16)
    key_block[160:168, :] = jnp.concatenate([jnp.ones_like(id_row), id_row, zeros], axis=0).astype(bf16)
    for copy in copies[1:]:
        copy.wait()


def pack(queries, keys, values, ids):
    count = queries.shape[1]
    return pl.pallas_call(
        pack_kernel,
        out_shape=[
            jax.ShapeDtypeStruct((88, count), bf16),
            jax.ShapeDtypeStruct((168, count), bf16),
        ],
        in_specs=[pl.BlockSpec(memory_space=pltpu.HBM)] * 4,
        out_specs=[IN_VMEM] * 2,
        scratch_shapes=[pltpu.VMEM((1, count), jnp.int32), pltpu.SemaphoreType.DMA((4,))],
        compiler_params=pltpu.CompilerParams(vmem_limit_bytes=4 << 20),
        name="pack",
    )(*(pltpu.with_memory_space_constraint(x, pltpu.HBM) for x in (queries, keys, values, ids)))


def attend_block(query, held_k, held_v, limits, which, row_max, total, excess):
    count = query.shape[1]
    tiles, sub = 2, 256
    q_low, q_high = limits[which, 0], limits[which, 3]

    def tile(kb, start, tile_keys, masked, raising, low=None, high=None, pick=None):
        rows = pl.ds(start, tile_keys)
        key_tile = held_k[kb, rows, :]
        value_tile = held_v[kb, :, rows]
        if masked:
            key_ids = jnp.broadcast_to(value_tile[80:88, :].T.astype(f32)[:, 1:2], (tile_keys, sub))

        def score(j):
            columns = slice(j * sub, (j + 1) * sub)
            found = jnp.dot(key_tile, query[0:80, columns], preferred_element_type=f32)
            if masked:
                query_ids = query[80:88, columns].astype(f32)[0:1, :]
                found = jnp.where(key_ids == query_ids, found, MASKED)
            return found

        def part(j, scores):
            columns = slice(j * sub, (j + 1) * sub)
            old = row_max[:, columns]
            if raising:
                new = jnp.maximum(old, jnp.max(scores, axis=0, keepdims=True))
                weights = jnp.exp2((scores - new) * EXP2_SCALE).astype(bf16)
                rescale = jnp.exp2((old - new) * EXP2_SCALE)
                total[:, columns] = total[:, columns] * rescale + jnp.dot(
                    value_tile, weights, preferred_element_type=f32
                )
                row_max[:, columns] = new
            else:
                weights = jnp.exp2((scores - old) * EXP2_SCALE).astype(bf16)
                total[:, columns] = total[:, columns] + jnp.dot(
                    value_tile, weights, preferred_element_type=f32
                )
                above = jnp.max(scores, axis=0, keepdims=True) - old
                excess[:, columns] = jnp.maximum(excess[:, columns], above)

        if pick is not None:
            part(pick, score(pick))
            return
        if low is not None:
            for j in range(count // sub):
                overlaps = jnp.logical_and(
                    low <= limits[which, 5 + 2 * j], high >= limits[which, 4 + 2 * j]
                )

                @pl.when(overlaps)
                def _():
                    part(j, score(j))

            return
        scores = score(0)
        for j in range(count // sub):
            following = score(j + 1) if (j + 1) * sub < count else None
            part(j, scores)
            scores = following

    def every_key_block(keep_shift):
        row_max[...] = jnp.full_like(row_max, NO_MAX)
        total[...] = jnp.zeros_like(total)
        excess[...] = jnp.zeros_like(excess)

        def key_block_step(kb, started):
            low, high = limits[4 + kb, 0], limits[4 + kb, 3]
            live = jnp.logical_and(low <= q_high, high >= q_low)
            pure = q_low == q_high
            still = jnp.logical_and(
                jnp.logical_and(pure, jnp.logical_and(low == high, low == q_low)), keep_shift
            )

            @pl.when(jnp.logical_and(still, started == 0))
            def _():
                for j in range(count // sub):
                    columns = slice(j * sub, (j + 1) * sub)
                    found = jnp.dot(held_k[kb, 0:128, :], query[0:80, columns], preferred_element_type=f32)
                    row_max[:, columns] = jnp.max(found, axis=0, keepdims=True)

            @pl.when(still)
            def _():
                tile(kb, 0, count, False, False)

            by_part = jnp.logical_and(
                jnp.logical_and(live, jnp.logical_not(pure)), jnp.logical_and(low == high, keep_shift)
            )
            reached = started
            for j in range(count // sub):
                part_low, part_high = limits[which, 4 + 2 * j], limits[which, 5 + 2 * j]
                one = part_low == part_high
                meets = jnp.logical_and(low <= part_high, high >= part_low)
                same = jnp.logical_and(by_part, jnp.logical_and(one, meets))
                fresh = jnp.bitwise_and(started, 1 << j) == 0
                columns = slice(j * sub, (j + 1) * sub)

                @pl.when(jnp.logical_and(same, fresh))
                def _():
                    found = jnp.dot(held_k[kb, 0:128, :], query[0:80, columns], preferred_element_type=f32)
                    row_max[:, columns] = jnp.max(found, axis=0, keepdims=True)

                @pl.when(same)
                def _():
                    tile(kb, 0, count, False, False, pick=j)

                @pl.when(jnp.logical_and(by_part, jnp.logical_and(meets, jnp.logical_not(one))))
                def _():
                    for t in range(tiles):
                        tile(kb, t * (count // tiles), count // tiles, True, True, pick=j)

                reached = jnp.bitwise_or(
                    reached, jnp.logical_and(one, meets).astype(jnp.int32) * (1 << j)
                )

            @pl.when(
                jnp.logical_and(live, jnp.logical_not(jnp.logical_or(still, by_part)))
            )
            def _():
                def half(t, unused):
                    low, high = limits[4 + kb, 2 * t], limits[4 + kb, 2 * t + 1]

                    touches = jnp.logical_and(low <= q_high, high >= q_low)
                    begin = pl.multiple_of(t * (count // tiles), 128)

                    @pl.when(jnp.logical_and(touches, pure))
                    def _():
                        tile(kb, begin, count // tiles, True, True)

                    @pl.when(jnp.logical_and(touches, jnp.logical_not(pure)))
                    def _():
                        tile(kb, begin, count // tiles, True, True, low, high)

                    return 0

                lax.fori_loop(0, tiles, half, 0)

            return reached

        lax.fori_loop(0, 4, key_block_step, 0)

    def attempt(tried, unused):
        @pl.when(jnp.logical_or(tried == 0, jnp.max(excess[...]) > MOST_EXCESS))
        def _():
            every_key_block(tried == 0)

        return 0

    lax.fori_loop(0, 2, attempt, 0)


def store_partial(out, row_max, total):
    def split(value, parts):
        pieces = []
        for _ in range(parts):
            piece = value.astype(bf16).astype(f32)
            pieces.append(piece)
            value = value - piece
        return pieces

    rows = split(total[80:81, :], 2) + split(row_max[...], 3)
    rows.append(jnp.zeros((3, out.shape[1]), f32))
    out[0:80, :] = total[0:80, :].astype(bf16)
    out[80:88, :] = jnp.concatenate(rows, axis=0).astype(bf16)


def find_limits(ids, limits, limits_s, sem):
    count = ids.shape[1]
    lane = lax.broadcasted_iota(jnp.int32, (8, 128), 1)
    table = jnp.zeros((8, 128), f32)
    for t in range(2):
        part = ids[:, t * (count // 2) : (t + 1) * (count // 2)]
        table = jnp.where(lane == 2 * t, jnp.min(part, axis=1, keepdims=True), table)
        table = jnp.where(lane == 2 * t + 1, jnp.max(part, axis=1, keepdims=True), table)
    for t in range(4):
        part = ids[:, t * (count // 4) : (t + 1) * (count // 4)]
        table = jnp.where(lane == 4 + 2 * t, jnp.min(part, axis=1, keepdims=True), table)
        table = jnp.where(lane == 5 + 2 * t, jnp.max(part, axis=1, keepdims=True), table)
    limits[...] = table.astype(jnp.int32)
    copy = pltpu.make_async_copy(limits, limits_s, sem)
    copy.start()
    copy.wait()


def attend_kernel(blocks, first, *refs):
    queries, refs = refs[:blocks], refs[blocks:]
    if first:
        key_values, refs = refs[:4], refs[4:]
    else:
        (held_k, held_v), refs = refs[:2], refs[2:]
    outs, refs = refs[:blocks], refs[blocks:]
    if first:
        (held_k, held_v), refs = refs[:2], refs[2:]
    query, ids, limits, limits_s, row_max, total, excess, sem = refs
    ids[...] = jnp.zeros_like(ids)
    for i in range(4):
        if first:
            held_k[i] = key_values[i][0:80, :].T
            held_v[i] = key_values[i][80:168, :]
        ids[4 + i : 5 + i, :] = held_v[i, 80:88, :].astype(f32)[1:2, :]
    for i in range(blocks):
        query[i] = queries[i][...]
        ids[i : i + 1, :] = queries[i][80:88, :].astype(f32)[0:1, :]
    find_limits(ids, limits, limits_s, sem)

    def one(i, unused):
        attend_block(query.at[i], held_k, held_v, limits_s, i, row_max, total, excess)
        for o in range(blocks):

            @pl.when(i == o)
            def _():
                store_partial(outs[o], row_max, total)

        return 0

    lax.fori_loop(0, blocks, one, 0)


def attend(queries, key_values, held=None):
    count = queries[0].shape[1]
    first = held is None
    shapes = [jax.ShapeDtypeStruct((88, count), bf16)] * len(queries)
    if first:
        shapes.append(jax.ShapeDtypeStruct((4, count, 80), bf16))
        shapes.append(jax.ShapeDtypeStruct((4, 88, count), bf16))
    operands = list(queries) + list(key_values if first else held)
    out = pl.pallas_call(
        functools.partial(attend_kernel, len(queries), first),
        out_shape=shapes,
        in_specs=[IN_VMEM] * len(operands),
        out_specs=[IN_VMEM] * len(shapes),
        scratch_shapes=[
            pltpu.VMEM((len(queries), 88, count), bf16),
            pltpu.VMEM((8, count), f32),
            pltpu.VMEM((8, 128), jnp.int32),
            pltpu.SMEM((8, 128), jnp.int32),
            pltpu.VMEM((1, count), f32),
            pltpu.VMEM((88, count), f32),
            pltpu.VMEM((1, count), f32),
            pltpu.SemaphoreType.DMA,
        ],
        compiler_params=pltpu.CompilerParams(vmem_limit_bytes=16 << 20),
        name="attend_first" if first else "attend_next",
    )(*operands)
    return list(out[: len(queries)]), list(out[len(queries) :])


def this_core():
    return lax.rem(lax.axis_index("section"), 2)


def combine_kernel(*refs):
    parts, (mine, others, whole) = refs[:4], refs[4:]
    core = this_core()
    sums, maxima = [], []
    for part in parts:
        rows = part[80:88, :].astype(f32)
        sums.append(rows[0:1, :] + rows[1:2, :])
        maxima.append((rows[2:3, :] + rows[3:4, :]) + rows[4:5, :])
    top = functools.reduce(jnp.maximum, maxima)
    factors = [jnp.exp2((m - top) * EXP2_SCALE) for m in maxima]
    inverse = 1.0 / functools.reduce(jnp.add, [w * s for w, s in zip(factors, sums)])
    mixed = functools.reduce(
        jnp.add, [part[0:80, :].astype(f32) * w for part, w in zip(parts, factors)]
    )
    whole[...] = (mixed * inverse).astype(bf16)
    half = mine.shape[1]
    mine[...] = whole[:, pl.ds(pl.multiple_of(core * half, 128), half)]
    others[...] = whole[:, pl.ds(pl.multiple_of((1 - core) * half, 128), half)]


def combine(parts):
    count = parts[0].shape[1]
    return pl.pallas_call(
        combine_kernel,
        out_shape=[jax.ShapeDtypeStruct((80, count // 2), bf16)] * 2,
        in_specs=[IN_VMEM] * 4,
        out_specs=[IN_VMEM] * 2,
        scratch_shapes=[pltpu.VMEM((80, count), bf16)],
        compiler_params=pltpu.CompilerParams(vmem_limit_bytes=6 << 20),
        name="combine",
    )(*parts)


def copies_kernel(moves, *refs):
    sources, whole, sems = refs[:-2], refs[-2], refs[-1]
    copies = []
    for i, (source, start, target, rows) in enumerate(moves):
        copies.append(
            pltpu.make_async_copy(
                sources[source].at[start : start + rows, :],
                whole.at[target : target + rows, :],
                sems.at[i],
            )
        )
        copies[-1].start()
    for copy in copies:
        copy.wait()


def place_rows(sources, moves, name, spaces=None):
    rows = sum(move[3] for move in moves)
    return pl.pallas_call(
        functools.partial(copies_kernel, moves),
        out_shape=jax.ShapeDtypeStruct((rows, sources[0].shape[1]), bf16),
        in_specs=[pl.BlockSpec(memory_space=space) for space in spaces or [pl.ANY] * len(sources)],
        out_specs=IN_VMEM,
        scratch_shapes=[pltpu.SemaphoreType.DMA((len(moves),))],
        compiler_params=pltpu.CompilerParams(vmem_limit_bytes=5 << 20),
        name=name,
    )(*sources)


def project_kernel(*refs):
    pieces = refs[:8]
    (weight, gain, shift, *projs, out_mine, out_others, normed) = refs[8:]
    width = weight.shape[1]
    count = pieces[0].shape[1]
    attended = jnp.concatenate([piece[...] for piece in pieces], axis=0)
    rows = jnp.dot(attended.T, weight[...], preferred_element_type=f32).astype(bf16).astype(f32)
    rows = rows - jnp.sum(rows, axis=1, keepdims=True) * (1.0 / width)
    spread = jnp.sum(rows * rows, axis=1, keepdims=True) * (1.0 / width)
    rows = rows * lax.rsqrt(spread + EPSILON) * gain[...] + shift[...]
    for k in range(width // 128):
        normed[k] = rows[:, k * 128 : (k + 1) * 128]
    tokens = []
    for r in range(4):
        every_fourth = pl.ds(r, count // 4, stride=4)
        tokens.append(
            jnp.concatenate(
                [normed[k, every_fourth, :].astype(bf16) for k in range(width // 128)], axis=1
            )
        )
    for out, proj in ((out_others, projs[1]), (out_mine, projs[0])):
        linear = jnp.zeros(out.shape, f32)
        for r in range(4):
            linear = linear + lax.dot_general(
                proj[:, r * width : (r + 1) * width],
                tokens[r],
                (((1,), (1,)), ((), ())),
                preferred_element_type=f32,
            )
        out[...] = linear


def project(pieces, weight, gain, shift, mine, others):
    count, width = pieces[0].shape[1], weight.shape[1]
    return pl.pallas_call(
        project_kernel,
        out_shape=[jax.ShapeDtypeStruct((mine.shape[0], count // 4), f32)] * 2,
        in_specs=[IN_VMEM] * 13,
        out_specs=[IN_VMEM] * 2,
        scratch_shapes=[pltpu.VMEM((width // 128, count, 128), f32)],
        compiler_params=pltpu.CompilerParams(vmem_limit_bytes=24 << 20),
        name="project",
    )(*pieces, weight, gain, shift, mine, others)


def finish_kernel(mine, rest, bias, out):
    core, count = this_core(), mine.shape[1]
    bias_column = jnp.broadcast_to(bias[...], (8, mine.shape[0])).T[:, 0:1]
    for place, product in ((core, mine), (1 - core, rest)):
        linear = product[...] + bias_column
        active = 0.5 * linear * (1.0 + lax.erf(linear * (0.5**0.5)))
        out[:, pl.ds(pl.multiple_of(place * count, 128), count)] = active.astype(bf16)


def finish(mine, rest, bias):
    rows, count = mine.shape
    return pl.pallas_call(
        finish_kernel,
        out_shape=jax.ShapeDtypeStruct((rows, 2 * count), bf16),
        in_specs=[IN_VMEM] * 3,
        out_specs=IN_VMEM,
        compiler_params=pltpu.CompilerParams(vmem_limit_bytes=4 << 20),
        name="finish",
    )(mine, rest, bias)


def on_device(
    queries, keys, values, segment_ids, out_weight, norm_gain, norm_bias, proj_weight, proj_bias
):
    blocks = lax.axis_size("blk")
    query_block, key_block = pack(queries.T, keys.T, values.T, segment_ids[None, :])

    sections = lax.axis_size("section")

    def swap(block, mask):
        if mask == 0:
            return block
        perm = []
        for i in range(blocks):
            for section in range(sections):
                turn = section % 2
                y, z = i // 8 ^ mask >> 3, ((i % 8 - turn) % 8 ^ mask & 7) + turn
                perm.append((i * sections + section, (y * 8 + z % 8) * sections + section))
        return lax.ppermute(block, ("blk", "section"), perm)

    def send(block, to):
        perm = []
        for x in range(4):
            for c in range(2):
                for t in range(2):
                    a, b, d = to(x, c, t)
                    perm.append(((x * 2 + c) * 2 + t, (a % 4 * 2 + b) * 2 + d))
        return lax.ppermute(block, GROUP, perm)

    def across(x, c, t):
        return x, 1 - c, t

    others = send(proj_weight.T, across)
    key_blocks = [swap(key_block, mask) for mask in KEY_PARTNERS]
    queries_at = [query_block, swap(query_block, QUERY_PARTNERS[1])]
    late_query, late_weight, others, _ = lax.optimization_barrier(
        (query_block, out_weight, others, (key_blocks, queries_at[1]))
    )
    queries_at += [swap(late_query, mask) for mask in QUERY_PARTNERS[2:]]
    far = send(late_weight, lambda x, c, t: (x, c, 1 - t))
    (first,), held = attend([queries_at[1]], key_blocks)
    both = place_rows(
        [pltpu.with_memory_space_constraint(late_weight, pltpu.HBM), far],
        [(i, 0, i * HDIM, HDIM) for i in range(2)],
        "both",
        (pltpu.HBM, pl.ANY),
    )
    first = swap(first, QUERY_PARTNERS[1])
    both, late_queries, held = lax.optimization_barrier((both, queries_at[2:], held))
    steps = (1, 3, 2)
    weights = [both] + [send(both, lambda x, c, t, d=d: (x + d, c, t)) for d in steps]
    late, _ = attend(late_queries, None, held)
    late, first = lax.optimization_barrier((late, first))
    own_query, _ = lax.optimization_barrier((query_block, late))
    (own,), _ = attend([own_query], None, held)
    returned = [own, first] + [swap(part, mask) for part, mask in zip(late, QUERY_PARTNERS[2:])]
    weights, returned[0] = lax.optimization_barrier((weights, own))
    half = place_rows(weights, [(i, 0, i * 160, 160) for i in range(4)], "assemble")
    returned, half = lax.optimization_barrier((returned, half))
    other_half = send(half, across)
    kept, given = combine(returned)

    pair = place_rows([kept, send(given, across)], [(i, 0, i * HDIM, HDIM) for i in range(2)], "pair")
    pieces = {(0, 0): pair, (0, 1): send(pair, lambda x, c, t: (x, c, 1 - t))}
    for e in (0, 1):
        for d in (2, 1, 3):
            pieces[d, e] = send(pieces[0, e], lambda x, c, t: (x + d, c, t))
    order = [(d, e) for d in (0,) + steps for e in (0, 1)]
    moves = [(h, i * HDIM, (2 * i + h) * HDIM, HDIM) for i in range(8) for h in range(2)]
    weight = place_rows([half, other_half], moves, "join")
    out_mine, out_others = project(
        [pieces[place] for place in order],
        weight,
        norm_gain[None, :],
        norm_bias[None, :],
        proj_weight.T,
        others,
    )
    return finish(out_mine, send(out_others, across), proj_bias[None, :]).T


def solution(mesh):
    placed = (
        P("blk", GROUP),
        P("blk", GROUP),
        P("blk", GROUP),
        P("blk"),
        P(GROUP, None),
        P(),
        P(),
        P(None, GROUP),
        P(GROUP),
    )
    return jax.shard_map(
        on_device,
        mesh=mesh,
        in_specs=placed,
        out_specs=P("blk", GROUP),
        check_vma=False,
    )
```
